32 devices in a mesh: groups: 2 (over y), tile: 16 (over z, x, core).
Axes of the slice: x: 2, y: 2, z: 4, core: 2. Of those that a mesh axis runs over, the one named last changes fastest.
Arguments:
- sar_faces: bfloat16 [512, 8, 128], P(('groups', 'tile')), parts along dimension 0, may hold values from -6 to 6
- dest_owner: int32 [512, 1], P(('groups', 'tile')), parts along dimension 0, may hold values from 0 to 15; in each aligned block of 16 rows (0 to 15, 16 to 31, ...) at most 2 rows name the same one
- face_slot: int32 [512], P(('groups', 'tile')), parts along dimension 0, may hold values from 0 to 31
- valid_pixels: int32 [512], P(('groups', 'tile')), parts along dimension 0, may hold values from 1 to 8
- cloud_mask: int32 [32, 256], P(('groups', 'tile')), parts along dimension 0, may hold values 0 or 1
- time_index: int32 [32], P(('groups', 'tile')), parts along dimension 0, may hold values from 0 to 999
- clean_latent: bfloat16 [32, 256, 384], P(('groups', 'tile')), parts along dimension 0, may hold values from -6 to 6
- noise_latent: bfloat16 [32, 256, 384], P(('groups', 'tile')), parts along dimension 0, may hold values from -6 to 6
- encoder_first: bfloat16 [3, 8, 16, 48], replicated, may hold values from -0.875 to 0.875
- encoder_second: bfloat16 [3, 8, 48, 48], replicated, may hold values from -0.5 to 0.5
- conv_kernel: bfloat16 [9, 384, 384], replicated, may hold values from -0.109375 to 0.109375
- norm_gain: float32 [384], replicated, may hold values from 0.5 to 2
Outputs:
- grad_kernel: float32 [18, 384, 384], P('groups'), parts along dimension 0
- grad_gain: float32 [768], P('groups'), parts along dimension 0
- grad_first: float32 [6, 8, 16, 48], P('groups'), parts along dimension 0
- grad_second: float32 [6, 8, 48, 48], P('groups'), parts along dimension 0
The draws below stay inside these ranges and needn't reach their ends.
There are 2 independent parts, one for each index of `groups`. The reference program is written for one: setup_inputs(seed, part) draws one part's arguments, and reference() takes and returns one part's arrays. A program takes and returns all parts, laid end to end along the dimension named above; an argument that names none is the same for every part. Nothing has to cross between parts.
Inputs may be any that keep to these rules, and one draw needn't show every extreme that they name: `dest_owner`: among each device's 16 faces, at most 2 name one tile owner.
All inputs are finite; a program needn't handle non-finite values. No bound on the sum of `cloud_mask` on one device may be relied on, other than what follows from the above.
Results may differ from the reference program's by a relative error of at most 0.0038.
Values may be sent and summed in bfloat16 or wider, within the bound.
A program may use at most 64 MiB of HBM per device.

```python
import math
import jax
import jax.numpy as jnp
import numpy as np
from jax import lax

C = 384
CIN = 128
G = 8
LINE = 8
MOST = 2
COLS = 256
NSTEPS = 1000
FACES_DEV = 16
TILES = 16
SCENE_ROWS = 16
FACES = 256
TILE_FACES = 32
N_TILE = 16


def plant(drawn, key, low, largest):
    shape = drawn.shape
    spot = [jax.random.randint(jax.random.fold_in(key, axis), (), 0, shape[axis]) for axis in range(len(shape))]
    drawn = drawn.at[tuple(spot)].set(low)
    longest = shape.index(max(shape))
    spot[longest] = (spot[longest] + 1) % shape[longest]
    return drawn.at[tuple(spot)].set(largest)


def block_scale(key, extent, split, low, largest):
    def one(dim, blocks):
        steps = jax.random.uniform(jax.random.fold_in(jax.random.fold_in(key, 6), dim), (blocks,), jnp.float32, low / len(split), largest / len(split))
        return jnp.repeat(jnp.exp(steps), extent[dim] // blocks).reshape((-1,) + (1,) * (len(extent) - dim - 1))

    factor_of = one(*split[0])
    for cut in split[1:]:
        factor_of = factor_of * one(*cut)
    return factor_of


def routed_block(stream_key, own, number, rows, number_of, top, most, lean):
    sequence = jax.random.permutation(stream_key, number_of)
    packed, usual = load_shares(number_of, rows * top, most, lean, True), load_shares(number_of, rows * top, most, lean, False)
    places = jnp.arange(number_of)

    def named(tallies, rotation):
        used = int((tallies > 0).sum())
        fixed = max(1, used // 4)
        moved = fixed + (places - fixed + rotation * (used - fixed)) % max(1, number_of - fixed)
        return jnp.zeros((number_of,), jnp.int32).at[sequence[jnp.where(places < fixed, places, moved)]].set(jnp.asarray(tallies, jnp.int32))

    tallies = jnp.where(number % 4 == 0, named(packed, number // 4), named(usual, number - number // 4 - 1))
    mixed = jax.random.permutation(jax.random.fold_in(own, 3), number_of)
    giver, receiver = mixed[0:number_of // 2 * 2:2], mixed[1:number_of // 2 * 2:2]
    room = jnp.minimum(tallies[giver] - 1, most - tallies[receiver]) // 2
    room = jnp.where((giver == sequence[0]) | (receiver == sequence[0]) | (tallies[receiver] == 0), 0, jnp.maximum(room, 0))
    moved = jax.random.randint(jax.random.fold_in(own, 4), (number_of // 2,), 0, 1 << 20) % (room + 1)
    tallies = tallies.at[giver].add(-moved).at[receiver].add(moved)
    items = jnp.searchsorted(jnp.cumsum(tallies), jnp.arange(rows * top), side="right").astype(jnp.int32)
    table = items.reshape(top, rows).T
    table = table[jax.random.permutation(jax.random.fold_in(own, 1), rows)]
    rotation = jax.random.randint(jax.random.fold_in(own, 2), (rows, 1), 0, top)
    return jnp.take_along_axis(table, (jnp.arange(top)[None, :] + rotation) % top, axis=1)


def load_shares(amount, total, bound, lean, full):
    weights = [(1 << 20) // math.isqrt(standing ** lean) + 1 for standing in range(1, amount + 1)]
    largest = bound if full else min(bound, max(-(-total // amount), total * weights[0] // sum(weights)))
    least = 1 if total - largest >= amount - 1 else 0
    counts, surplus = [largest] + [least] * (amount - 1), total - largest - least * (amount - 1)
    while surplus > 0:
        free = [i for i in range(1, amount) if counts[i] < largest] or [i for i in range(1, amount) if counts[i] < bound]
        pool, left = sum([weights[i] for i in free]), surplus
        for i in free:
            extra = min(bound - counts[i], max(1, left * weights[i] // pool), surplus)
            counts[i] = counts[i] + extra
            surplus = surplus - extra
    return np.array(counts)


def noise(stream_key, shape, scale, limit, cuts=(), kind=jnp.bfloat16):
    result = scale * jax.random.normal(stream_key, shape, jnp.float32)
    if cuts:
        result = result * block_scale(stream_key, shape, cuts, -0.22, 0.18)
    return jnp.clip(result, -limit, limit).astype(kind)


def setup_inputs(seed: int = 0, part: int = 0) -> dict:
    seeds = jax.random.split(jax.random.key(seed), 13)
    own_keys = jax.random.split(jax.random.fold_in(seeds[12], part), 13)
    sar_faces = noise(own_keys[0], (FACES, LINE, CIN), 1.0, 6.0, ((0, 16),))
    dest_owner_keys = jax.random.split(jax.random.fold_in(own_keys[1], 1), FACES // FACES_DEV)
    dest_owner_turns = jax.random.permutation(jax.random.fold_in(own_keys[1], 3), FACES // FACES_DEV)
    dest_owner = jax.vmap(lambda own, number: routed_block(jax.random.fold_in(own_keys[1], 2), own, number, FACES_DEV, N_TILE, 1, MOST, 2))(dest_owner_keys, dest_owner_turns).reshape((FACES, 1))
    face_slot = plant(jax.random.randint(own_keys[2], (FACES,), 0, TILE_FACES), jax.random.fold_in(own_keys[2], 1), 0, TILE_FACES - 1).astype(jnp.int32)
    valid_pixels = plant(jax.random.randint(own_keys[3], (FACES,), 1, LINE + 1), jax.random.fold_in(own_keys[3], 1), 1, LINE).astype(jnp.int32)
    cloud_mask = plant((jax.random.randint(own_keys[4], (SCENE_ROWS, COLS), 0, 3) < 1).astype(jnp.int32), jax.random.fold_in(own_keys[4], 1), 0, 1)
    time_index = plant(jax.random.randint(own_keys[5], (TILES,), 0, NSTEPS), jax.random.fold_in(own_keys[5], 1), 0, NSTEPS - 1).astype(jnp.int32)
    clean_latent = noise(own_keys[6], (SCENE_ROWS, COLS, C), 1.0, 6.0, ((0, 16),))
    noise_latent = noise(own_keys[7], (SCENE_ROWS, COLS, C), 1.0, 6.0, ((0, 16),))
    encoder_first = noise(seeds[8], (3, G, CIN // G, C // G), (3 * CIN // G) ** -0.5, 0.875)
    encoder_second = noise(seeds[9], (3, G, C // G, C // G), (3 * C // G) ** -0.5, 0.5)
    conv_kernel = noise(seeds[10], (9, C, C), (9 * C) ** -0.5, 0.109375)
    norm_gain = jnp.clip(jnp.exp(jax.random.uniform(seeds[11], (C,), jnp.float32, math.log(0.5), math.log(2.0))), 0.5, 2.0)
    return {"sar_faces": sar_faces, "dest_owner": dest_owner, "face_slot": face_slot, "valid_pixels": valid_pixels, "cloud_mask": cloud_mask, "time_index": time_index, "clean_latent": clean_latent, "noise_latent": noise_latent, "encoder_first": encoder_first, "encoder_second": encoder_second, "conv_kernel": conv_kernel, "norm_gain": norm_gain}


highest = lax.Precision.HIGHEST
epsilon = 1e-06

def shift_line(values, offset):
    if offset == 0:
        return values
    zeros = jnp.zeros_like(values[:, :abs(offset)])
    if offset > 0:
        return jnp.concatenate([values[:, offset:], zeros], axis=1)
    return jnp.concatenate([zeros, values[:, :offset]], axis=1)

def grouped_taps(inputs, weight, spread):
    summed = jnp.zeros(inputs.shape[:3] + (weight.shape[-1],), jnp.float32)
    for shift_tap in range(3):
        shifted = shift_line(inputs, (shift_tap - 1) * spread)
        summed = summed + jnp.einsum('flgi,gio->flgo', shifted, weight[shift_tap], precision=highest)
    return summed

def encoder(sar_faces, first_w, second_w):
    face_count, length, channels_in = sar_faces.shape
    groups = first_w.shape[1]
    inputs = sar_faces.astype(jnp.float32).reshape(face_count, length, groups, -1)
    hidden = jax.nn.silu(grouped_taps(inputs, first_w, 1)).reshape(face_count, length, -1)
    hidden = lax.optimization_barrier(hidden.astype(jnp.bfloat16)).astype(jnp.float32)
    second = grouped_taps(hidden.reshape(face_count, length, groups, -1), second_w, 2)
    return (hidden + second.reshape(face_count, length, -1)).astype(jnp.bfloat16)

def convolve_forward(padded, kernel, rows, columns):
    channels = kernel.shape[-1]
    summed = jnp.zeros((rows * columns, channels), jnp.float32)
    for row_tap in range(3):
        for col_tap in range(3):
            window = padded[row_tap:row_tap + rows, col_tap:col_tap + columns].reshape(-1, channels)
            summed = summed + jnp.dot(window, kernel[3 * row_tap + col_tap], preferred_element_type=jnp.float32)
    return summed

def convolve_backward(padded_act, padded_grad, kernel, rows, columns):
    channels = kernel.shape[-1]
    incoming = padded_grad[1:rows + 1, 1:columns + 1].reshape(-1, channels)
    flows = jnp.zeros((rows * columns, channels), jnp.float32)
    kernels = []
    for row_tap in range(3):
        for col_tap in range(3):
            window = padded_act[row_tap:row_tap + rows, col_tap:col_tap + columns].reshape(-1, channels)
            kernels.append(lax.dot_general(window, incoming, (((0,), (0,)), ((), ())), preferred_element_type=jnp.float32))
            moved = padded_grad[2 - row_tap:2 - row_tap + rows, 2 - col_tap:2 - col_tap + columns].reshape(-1, channels)
            flows = flows + lax.dot_general(moved, kernel[3 * row_tap + col_tap], (((1,), (1,)), ((), ())), preferred_element_type=jnp.float32)
    return (flows, jnp.stack(kernels))

def norm_backward(flows, lifted, normed, inverse, gain):
    logistic = jax.nn.sigmoid(lifted)
    grad_lift = flows * logistic * (1.0 + lifted * (1.0 - logistic))
    gain_part = lax.optimization_barrier(jnp.sum(grad_lift * normed, axis=0))
    grad_norm = grad_lift * gain
    grad_hsum = inverse * (grad_norm - normed * lax.optimization_barrier(jnp.mean(grad_norm * normed, axis=-1, keepdims=True)))
    return (gain_part, grad_hsum)

def reference(sar_faces, dest_owner, face_slot, valid_pixels, cloud_mask, time_index, clean_latent, noise_latent, encoder_first, encoder_second, conv_kernel, norm_gain):
    first_w = encoder_first.astype(jnp.float32)
    second_w = encoder_second.astype(jnp.float32)
    encoded, pullback = jax.vjp(lambda one_w, two_w: encoder(sar_faces, one_w, two_w), first_w, second_w)
    length = sar_faces.shape[1]
    tile_count = time_index.shape[0]
    scene_rows, columns, channels = clean_latent.shape
    rows = scene_rows // tile_count
    tile_faces = rows * columns // length
    validity = (jnp.arange(length, dtype=jnp.int32)[None, :] < valid_pixels[:, None]).astype(jnp.float32)
    position = (dest_owner[:, 0] * tile_faces + face_slot).astype(jnp.int32)
    summed = jax.ops.segment_sum(encoded.astype(jnp.float32) * validity[..., None], position, num_segments=tile_count * tile_faces)
    covered = jax.ops.segment_sum(validity, position, num_segments=tile_count * tile_faces)
    covered = covered.reshape(-1, 1)
    condition = summed.reshape(-1, channels) / (1.0 + covered)
    time_value = (time_index.astype(jnp.float32) + 0.5) / NSTEPS
    time_rows = jnp.repeat(time_value, rows * columns)[:, None]
    noise_flat = noise_latent.astype(jnp.float32).reshape(-1, channels)
    clean_flat = clean_latent.astype(jnp.float32).reshape(-1, channels)
    hsum = (1.0 - time_rows) * noise_flat + time_rows * clean_flat + condition
    inverse = lax.rsqrt(lax.optimization_barrier(jnp.mean(hsum * hsum, axis=-1, keepdims=True)) + epsilon)
    normed = hsum * inverse
    lifted = normed * norm_gain
    activated = jax.nn.silu(lifted).astype(jnp.bfloat16).reshape(scene_rows, columns, channels)
    padded = jnp.pad(activated, ((1, 1), (1, 1), (0, 0)))
    predicted = convolve_forward(padded, conv_kernel, scene_rows, columns)
    pixel_weight = (1 + cloud_mask).astype(jnp.float32).reshape(-1, 1)
    grad_pred = (pixel_weight * (predicted - clean_flat + noise_flat) / (rows * columns)).astype(jnp.bfloat16)
    padded_grad = jnp.pad(grad_pred.reshape(scene_rows, columns, channels), ((1, 1), (1, 1), (0, 0)))
    flows, grad_kernel = convolve_backward(padded, padded_grad, conv_kernel, scene_rows, columns)
    grad_gain, grad_hsum = norm_backward(flows, lifted, normed, inverse, norm_gain)
    scaled = (grad_hsum / (1.0 + covered)).reshape(tile_count * tile_faces, length, channels)
    grad_face = (jnp.take(scaled, position, axis=0) * validity[..., None]).astype(jnp.bfloat16)
    grad_first, grad_second = pullback(grad_face)
    return (grad_kernel, grad_gain, grad_first, grad_second)
```

```python
import jax
import jax.numpy as jnp
from jax import lax
from jax.experimental import pallas as pl
from jax.experimental.pallas import tpu as pltpu
from jax.sharding import PartitionSpec as P

MOST = 2
NSTEPS = 1000


highest = lax.Precision.HIGHEST
epsilon = 1e-06


def with_halo(block, sides, width):
    for axis, dim in sides:
        count = lax.axis_size(axis)
        forward = [(i, i + 1) for i in range(count - 1)]
        backward = [(target, source) for source, target in forward]
        low = lax.ppermute(
            lax.slice_in_dim(block, block.shape[dim] - width, None, axis=dim), axis, forward
        )
        high = lax.ppermute(lax.slice_in_dim(block, 0, width, axis=dim), axis, backward)
        block = jnp.concatenate([low, block, high], axis=dim)
    return block


def shift_line(values, offset):
    if offset == 0:
        return values
    zeros = jnp.zeros_like(values[:, : abs(offset)])
    if offset > 0:
        return jnp.concatenate([values[:, offset:], zeros], axis=1)
    return jnp.concatenate([zeros, values[:, :offset]], axis=1)


def taps_forward(inputs, weight, spread):
    summed = jnp.zeros(inputs.shape[:3] + (weight.shape[-1],), jnp.float32)
    for shift_tap in range(3):
        shifted = shift_line(inputs, (shift_tap - 1) * spread)
        summed = summed + jnp.einsum(
            "flgi,gio->flgo", shifted, weight[shift_tap], preferred_element_type=jnp.float32
        )
    return summed


def taps_weight_grad(inputs, cotangent, spread, exact):
    pieces = []
    for shift_tap in range(3):
        shifted = shift_line(inputs, (shift_tap - 1) * spread)
        if exact:
            pieces.append(
                jnp.einsum(
                    "flgi,flgo->gio", shifted.astype(jnp.float32), cotangent, precision=highest
                )
            )
        else:
            pieces.append(
                jnp.einsum("flgi,flgo->gio", shifted, cotangent, preferred_element_type=jnp.float32)
            )
    return jnp.stack(pieces)


def taps_input_grad(cotangent, weight, spread):
    summed = jnp.zeros(cotangent.shape[:3] + (weight.shape[2],), jnp.float32)
    for shift_tap in range(3):
        moved = jnp.einsum(
            "flgo,gio->flgi", cotangent, weight[shift_tap], preferred_element_type=jnp.float32
        )
        summed = summed + shift_line(moved, -(shift_tap - 1) * spread)
    return summed


def encoder_forward(sar_faces, first_w, second_w):
    face_count, length, channels_in = sar_faces.shape
    groups = first_w.shape[1]
    inputs = sar_faces.reshape(face_count, length, groups, -1)
    first_out = taps_forward(inputs, first_w, 1)
    hidden = jax.nn.silu(first_out).astype(jnp.bfloat16)
    second = taps_forward(hidden, second_w, 2)
    encoded = (
        (hidden.astype(jnp.float32) + second).reshape(face_count, length, -1).astype(jnp.bfloat16)
    )
    return (encoded, (inputs, first_out, hidden))


def encoder_backward(saved, grad_face, first_w, second_w):
    inputs, first_out, hidden = saved
    groups = first_w.shape[1]
    face_count, length, channels = grad_face.shape
    cotangent = grad_face.reshape(face_count, length, groups, -1)
    second_part = taps_weight_grad(hidden, cotangent, 2, False)
    grad_hidden = cotangent.astype(jnp.float32) + taps_input_grad(cotangent, second_w, 2)
    logistic = jax.nn.sigmoid(first_out)
    grad_first_out = grad_hidden * logistic * (1.0 + first_out * (1.0 - logistic))
    first_part = taps_weight_grad(inputs, grad_first_out, 1, True)
    return (first_part, second_part)


def convolve_forward(padded, kernel, rows, columns):
    channels = kernel.shape[-1]
    summed = jnp.zeros((rows * columns, channels), jnp.float32)
    for row_tap in range(3):
        for col_tap in range(3):
            window = padded[row_tap : row_tap + rows, col_tap : col_tap + columns].reshape(
                -1, channels
            )
            summed = summed + jnp.dot(
                window, kernel[3 * row_tap + col_tap], preferred_element_type=jnp.float32
            )
    return summed


def convolve_backward(padded_act, padded_grad, kernel, rows, columns):
    channels = kernel.shape[-1]
    incoming = padded_grad[1 : rows + 1, 1 : columns + 1].reshape(-1, channels)
    flows = jnp.zeros((rows * columns, channels), jnp.float32)
    kernels = []
    for row_tap in range(3):
        for col_tap in range(3):
            window = padded_act[row_tap : row_tap + rows, col_tap : col_tap + columns].reshape(
                -1, channels
            )
            kernels.append(
                lax.dot_general(
                    window, incoming, (((0,), (0,)), ((), ())), preferred_element_type=jnp.float32
                )
            )
            moved = padded_grad[
                2 - row_tap : 2 - row_tap + rows, 2 - col_tap : 2 - col_tap + columns
            ].reshape(-1, channels)
            flows = flows + lax.dot_general(
                moved,
                kernel[3 * row_tap + col_tap],
                (((1,), (1,)), ((), ())),
                preferred_element_type=jnp.float32,
            )
    return (flows, jnp.stack(kernels))


def norm_backward(flows, lifted, normed, inverse, gain):
    logistic = jax.nn.sigmoid(lifted)
    grad_lift = flows * logistic * (1.0 + lifted * (1.0 - logistic))
    gain_part = jnp.sum(grad_lift * normed, axis=0)
    grad_norm = grad_lift * gain
    grad_hsum = inverse * (
        grad_norm - normed * jnp.mean(grad_norm * normed, axis=-1, keepdims=True)
    )
    return (gain_part, grad_hsum)


MESH = pl.DeviceIdType.MESH
VM = pltpu.VMEM


def entry_barrier(me, count):
    barrier = pltpu.get_barrier_semaphore()
    for k in range(1, count):
        pl.semaphore_signal(
            barrier, inc=1, device_id={"tile": lax.rem(me + k, count)}, device_id_type=MESH
        )
    pl.semaphore_wait(barrier, count - 1)


def exchange_kernel(count, x_ref, o_ref, send, recv, local):
    me = lax.axis_index("tile")
    entry_barrier(me, count)
    own = pltpu.make_async_copy(x_ref.at[me], o_ref.at[me], local)
    own.start()
    copies = []
    for k in range(1, count):
        to = lax.rem(me + k, count)
        copy = pltpu.make_async_remote_copy(
            src_ref=x_ref.at[to],
            dst_ref=o_ref.at[me],
            send_sem=send.at[k - 1],
            recv_sem=recv.at[k - 1],
            device_id={"tile": to},
            device_id_type=MESH,
        )
        copy.start()
        copies.append(copy)
    own.wait()
    for copy in copies:
        copy.wait()


def exchange(packed):
    count = packed.shape[0]
    return pl.pallas_call(
        lambda *refs: exchange_kernel(count, *refs),
        out_shape=jax.ShapeDtypeStruct(packed.shape, packed.dtype),
        in_specs=[pl.BlockSpec(memory_space=VM)],
        out_specs=pl.BlockSpec(memory_space=VM),
        scratch_shapes=[
            pltpu.SemaphoreType.DMA((count - 1,)),
            pltpu.SemaphoreType.DMA((count - 1,)),
            pltpu.SemaphoreType.DMA,
        ],
        compiler_params=pltpu.CompilerParams(collective_id=0, has_side_effects=True),
        name="exchange",
    )(packed)


class Gather:
    def __init__(self, buf, send, recv):
        self.buf, self.send_sem, self.recv_sem = buf, send, recv
        self.me = lax.axis_index("tile")
        self.core = lax.rem(self.me, 2)
        self.x = lax.rem(self.me // 2, 2)
        self.z = self.me // 4
        self.x_peer = self.z * 4 + (1 - self.x) * 2 + self.core
        self.sibling = self.z * 4 + self.x * 2 + (1 - self.core)

    def copy(self, chunk, to, index):
        return pltpu.make_async_remote_copy(
            src_ref=self.buf.at[chunk],
            dst_ref=self.buf.at[chunk],
            send_sem=self.send_sem.at[index],
            recv_sem=self.recv_sem.at[chunk],
            device_id={"tile": to},
            device_id_type=MESH,
        )

    def at(self, back, x, core):
        return lax.rem(self.z + 4 - back, 4) * 4 + x * 2 + core

    def start(self):
        self.copy(self.me, self.x_peer, 3).start()
        self.copy(self.me, self.sibling, 4).start()
        for k in (1, 3, 2):
            to = lax.rem(self.z + k, 4) * 4 + self.x * 2 + self.core
            self.copy(self.me, to, k - 1).start()

    def pass_z(self, back):
        chunk = self.at(back, self.x, self.core)
        self.copy(chunk, self.x_peer, 0).wait_recv()
        self.copy(chunk, self.x_peer, 5 + 2 * (back - 1)).start()
        self.copy(chunk, self.sibling, 6 + 2 * (back - 1)).start()

    def pass_x(self, back):
        chunk = self.at(back, 1 - self.x, self.core)
        self.copy(chunk, self.sibling, 0).wait_recv()
        self.copy(chunk, self.sibling, 11 + back).start()

    def take(self, back):
        for x in (self.x, 1 - self.x):
            chunk = self.at(back, x, 1 - self.core)
            self.copy(chunk, self.sibling, 0).wait_recv()

    def drain(self):
        for index in range(15):
            self.copy(self.me, self.sibling, index).wait_send()


def moved(values, offset, axis):
    extent = values.shape[axis]
    rolled = pltpu.roll(values, (-offset) % extent, axis)
    place = lax.broadcasted_iota(jnp.int32, values.shape, axis)
    return jnp.where(place == (extent - 1 if offset > 0 else 0), 0.0, rolled)


def halo_copies(src, halo, send, recv, me):
    up = pltpu.make_async_remote_copy(
        src_ref=src,
        dst_ref=halo.at[1],
        send_sem=send.at[0],
        recv_sem=recv.at[1],
        device_id={"tile": jnp.maximum(me - 1, 0)},
        device_id_type=MESH,
    )
    down = pltpu.make_async_remote_copy(
        src_ref=src,
        dst_ref=halo.at[0],
        send_sem=send.at[1],
        recv_sem=recv.at[0],
        device_id={"tile": jnp.minimum(me + 1, 15)},
        device_id_type=MESH,
    )
    return up, down


def middle_kernel(
    act_ref,
    clean_ref,
    noise_ref,
    weight_ref,
    kernel_ref,
    flows_ref,
    grad_ref,
    gathered_ref,
    halo_a,
    halo_g,
    gather_send,
    gather_recv,
    a_send,
    a_recv,
    g_send,
    g_recv,
):
    me = lax.axis_index("tile")
    last = 15
    columns = act_ref.shape[0]
    f32 = jnp.float32
    entry_barrier(me, 16)
    a_up, a_down = halo_copies(act_ref, halo_a, a_send, a_recv, me)
    g_up, g_down = halo_copies(grad_ref, halo_g, g_send, g_recv, me)

    @pl.when(me > 0)
    def _():
        a_up.start()

    @pl.when(me < last)
    def _():
        a_down.start()

    gathered_ref[me] = act_ref[...].T
    gather = Gather(gathered_ref, gather_send, gather_recv)
    gather.start()

    @pl.when(me == 0)
    def _():
        halo_a[0] = jnp.zeros_like(halo_a[0])
        halo_g[0] = jnp.zeros_like(halo_g[0])

    @pl.when(me == last)
    def _():
        halo_a[1] = jnp.zeros_like(halo_a[1])
        halo_g[1] = jnp.zeros_like(halo_g[1])

    own = act_ref[...]
    sums = [jnp.dot(own, kernel_ref[3 + d], preferred_element_type=f32) for d in range(3)]

    @pl.when(me > 0)
    def _():
        a_down.wait_recv()

    @pl.when(me < last)
    def _():
        a_up.wait_recv()

    above, below = halo_a[0], halo_a[1]
    sums = [
        sums[d]
        + jnp.dot(above, kernel_ref[d], preferred_element_type=f32)
        + jnp.dot(below, kernel_ref[6 + d], preferred_element_type=f32)
        for d in range(3)
    ]
    predicted = sums[1] + moved(sums[0], -1, 0) + moved(sums[2], 1, 0)
    grad = (
        weight_ref[...]
        * (predicted - clean_ref[...].astype(f32) + noise_ref[...].astype(f32))
        / columns
    ).astype(jnp.bfloat16)
    grad_ref[...] = grad

    @pl.when(me > 0)
    def _():
        g_up.start()

    @pl.when(me < last)
    def _():
        g_down.start()

    def back(values, tap):
        return lax.dot_general(
            values, kernel_ref[tap], (((1,), (1,)), ((), ())), preferred_element_type=f32
        )

    sums = [back(grad, 3 + d) for d in range(3)]
    for k in (1, 3, 2):
        gather.pass_z(k)

    @pl.when(me > 0)
    def _():
        g_down.wait_recv()

    @pl.when(me < last)
    def _():
        g_up.wait_recv()

    above, below = halo_g[0], halo_g[1]
    sums = [sums[d] + back(below, d) + back(above, 6 + d) for d in range(3)]
    flows_ref[...] = sums[1] + moved(sums[0], 1, 0) + moved(sums[2], -1, 0)
    for k in (0, 1, 3, 2):
        gather.pass_x(k)
    for k in (0, 1, 3, 2):
        gather.take(k)
    gather.drain()

    @pl.when(me > 0)
    def _():
        a_up.wait_send()
        g_up.wait_send()

    @pl.when(me < last)
    def _():
        a_down.wait_send()
        g_down.wait_send()


def middle(activated, clean, noise, pixel_weight, kernel):
    pixels, channels = activated.shape
    dma = pltpu.SemaphoreType.DMA
    return pl.pallas_call(
        middle_kernel,
        out_shape=(
            jax.ShapeDtypeStruct((pixels, channels), jnp.float32),
            jax.ShapeDtypeStruct((pixels, channels), jnp.bfloat16),
            jax.ShapeDtypeStruct((16, channels, pixels), jnp.bfloat16),
        ),
        in_specs=[pl.BlockSpec(memory_space=VM)] * 5,
        out_specs=(pl.BlockSpec(memory_space=VM),) * 3,
        scratch_shapes=[
            VM((2, pixels, channels), jnp.bfloat16),
            VM((2, pixels, channels), jnp.bfloat16),
            dma((15,)),
            dma((16,)),
            dma((2,)),
            dma((2,)),
            dma((2,)),
            dma((2,)),
        ],
        compiler_params=pltpu.CompilerParams(
            collective_id=1, has_side_effects=True, vmem_limit_bytes=40 * 2**20
        ),
        name="middle",
    )(activated, clean, noise, pixel_weight, kernel)


def outer_kernel(
    grad_ref, gathered_ref, result_ref, grads, shifted, gather_send, gather_recv
):
    me = lax.axis_index("tile")
    channels, pixels = gathered_ref.shape[1:]
    entry_barrier(me, 16)
    grads[me] = grad_ref[...]
    gather = Gather(grads, gather_send, gather_recv)
    gather.start()
    zeros = jnp.zeros((3, channels, pixels), jnp.bfloat16)
    shifted[:, :, 0:pixels] = zeros
    shifted[:, :, 17 * pixels : 18 * pixels] = zeros

    def shift_chunk(chunk):
        plain = gathered_ref[chunk]
        wide = plain.astype(jnp.float32)
        here = pl.ds(pl.multiple_of((chunk + 1) * pixels, pixels), pixels)
        shifted[0, :, here] = moved(wide, -1, 1).astype(jnp.bfloat16)
        shifted[1, :, here] = plain
        shifted[2, :, here] = moved(wide, 1, 1).astype(jnp.bfloat16)

    def shift_some(low, high):
        def step(i, carry):
            shift_chunk(i)
            return carry

        lax.fori_loop(low, high, step, 0)

    def multiply(back):
        base = lax.rem(gather.z + 4 - back, 4) * 4
        right = grads[pl.ds(base, 4)].reshape(4 * pixels, channels)

        def step(tap, carry):
            start = pl.multiple_of((base + tap // 3) * pixels, pixels)
            left = shifted[lax.rem(tap, 3), :, pl.ds(start, 4 * pixels)]
            product = jnp.dot(left, right, preferred_element_type=jnp.float32)
            if back == 0:
                result_ref[tap] = product
            else:
                result_ref[tap] = result_ref[tap] + product
            return carry

        lax.fori_loop(0, 9, step, 0)

    shift_some(0, 6)
    gather.pass_x(0)
    gather.pass_z(1)
    shift_some(6, 11)
    gather.pass_z(3)
    shift_some(11, 16)
    gather.pass_z(2)
    gather.take(0)
    multiply(0)
    for k in (1, 3, 2):
        gather.pass_x(k)
        gather.take(k)
        multiply(k)
    gather.drain()


def outer(grad, gathered):
    pixels, channels = grad.shape
    dma = pltpu.SemaphoreType.DMA
    return pl.pallas_call(
        outer_kernel,
        out_shape=jax.ShapeDtypeStruct((9, channels, channels), jnp.float32),
        in_specs=[pl.BlockSpec(memory_space=VM)] * 2,
        out_specs=pl.BlockSpec(memory_space=VM),
        scratch_shapes=[
            VM((16, pixels, channels), jnp.bfloat16),
            VM((3, channels, 18 * pixels), jnp.bfloat16),
            dma((15,)),
            dma((16,)),
        ],
        compiler_params=pltpu.CompilerParams(
            collective_id=2, has_side_effects=True, vmem_limit_bytes=48 * 2**20
        ),
        cost_estimate=pl.CostEstimate(
            flops=2 * 9 * 16 * pixels * channels * channels,
            bytes_accessed=20 * 2**20,
            transcendentals=0,
        ),
        name="outer",
    )(grad, gathered)


def body16(
    sar_faces,
    dest_owner,
    face_slot,
    valid_pixels,
    cloud_mask,
    time_index,
    clean_latent,
    noise_latent,
    encoder_first,
    encoder_second,
    conv_kernel,
    norm_gain,
):
    owners = lax.axis_size("tile")
    slot_total = owners * MOST
    face_count, length, channels_in = sar_faces.shape
    rows, columns, channels = clean_latent.shape
    tile_faces = rows * columns // length
    owner_list = dest_owner[:, 0]
    onehot = (owner_list[:, None] == jnp.arange(owners, dtype=jnp.int32)[None, :]).astype(jnp.int32)
    before = jnp.cumsum(onehot, axis=0) - onehot
    within = jnp.sum(before * onehot, axis=1)
    buffer_at = owner_list * MOST + within
    placed = (jnp.arange(slot_total, dtype=jnp.int32)[:, None] == buffer_at[None, :]).astype(
        jnp.int32
    )
    placer = placed.astype(jnp.bfloat16)
    labels = jnp.stack(
        [
            jnp.sum(placed * face_slot[None, :], axis=1),
            jnp.sum(placed * valid_pixels[None, :], axis=1),
        ],
        axis=-1,
    )
    packed = jnp.einsum(
        "sf,fjc->sjc", placer, sar_faces, preferred_element_type=jnp.float32
    ).astype(jnp.bfloat16)
    label_rows = jnp.pad(
        labels.astype(jnp.bfloat16)[:, None, :],
        ((0, 0), (0, length - 1), (0, channels_in - 2)),
    )
    arrived = exchange(
        jnp.concatenate([packed, label_rows], axis=1).reshape(
            owners, MOST * 2 * length, channels_in
        )
    ).reshape(slot_total, 2 * length, channels_in)
    raw_slots = arrived[:, :length]
    recv_labels = arrived[:, length, :2].astype(jnp.int32)
    received, saved = encoder_forward(raw_slots, encoder_first, encoder_second)
    recv_slot = recv_labels[:, 0]
    recv_count = recv_labels[:, 1]
    validity = (jnp.arange(length, dtype=jnp.int32)[None, :] < recv_count[:, None]).astype(
        jnp.float32
    )
    selector = recv_slot[:, None] == jnp.arange(tile_faces, dtype=jnp.int32)[None, :]
    masked = received * validity[..., None].astype(jnp.bfloat16)
    summed = jnp.einsum(
        "sp,sjc->pjc", selector.astype(jnp.bfloat16), masked, preferred_element_type=jnp.float32
    )
    covered = jnp.einsum(
        "sp,sj->pj", selector.astype(jnp.float32), validity, precision=highest
    ).reshape(-1, 1)
    condition = summed.reshape(-1, channels) / (1.0 + covered)
    time_value = (time_index[0].astype(jnp.float32) + 0.5) / NSTEPS
    noise_flat = noise_latent.astype(jnp.float32).reshape(-1, channels)
    clean_flat = clean_latent.astype(jnp.float32).reshape(-1, channels)
    hsum = (1.0 - time_value) * noise_flat + time_value * clean_flat + condition
    inverse = lax.rsqrt(jnp.mean(hsum * hsum, axis=-1, keepdims=True) + epsilon)
    normed = hsum * inverse
    lifted = normed * norm_gain
    activated = jax.nn.silu(lifted).astype(jnp.bfloat16)
    pixel_weight = (1 + cloud_mask).astype(jnp.float32).reshape(-1, 1)
    flows, grad_pred, gathered = middle(
        activated,
        clean_latent.reshape(-1, channels),
        noise_latent.reshape(-1, channels),
        pixel_weight,
        conv_kernel,
    )
    gain_part, grad_hsum = norm_backward(flows, lifted, normed, inverse, norm_gain)
    scaled = (grad_hsum / (1.0 + covered)).reshape(tile_faces, length, channels)
    slot_grads = (jnp.take(scaled, recv_slot, axis=0) * validity[..., None]).astype(jnp.bfloat16)
    first_part, second_part = encoder_backward(saved, slot_grads, encoder_first, encoder_second)
    parts = (gain_part, first_part, second_part)
    grad_pred, parts = lax.optimization_barrier((grad_pred, parts))
    reduced = lax.psum(parts, "tile")
    grad_kernel = outer(grad_pred, gathered)
    return (grad_kernel, reduced[0], reduced[1], reduced[2])


def body(
    sar_faces,
    dest_owner,
    face_slot,
    valid_pixels,
    cloud_mask,
    time_index,
    clean_latent,
    noise_latent,
    encoder_first,
    encoder_second,
    conv_kernel,
    norm_gain,
):
    owners = lax.axis_size("tile")
    slot_total = owners * MOST
    face_count, length, channels_in = sar_faces.shape
    rows, columns, channels = clean_latent.shape
    tile_faces = rows * columns // length
    owner_list = dest_owner[:, 0]
    onehot = (owner_list[:, None] == jnp.arange(owners, dtype=jnp.int32)[None, :]).astype(jnp.int32)
    before = jnp.cumsum(onehot, axis=0) - onehot
    within = jnp.sum(before * onehot, axis=1)
    buffer_at = owner_list * MOST + within
    placed = (jnp.arange(slot_total, dtype=jnp.int32)[:, None] == buffer_at[None, :]).astype(
        jnp.int32
    )
    placer = placed.astype(jnp.bfloat16)
    labels = jnp.stack(
        [
            jnp.sum(placed * face_slot[None, :], axis=1),
            jnp.sum(placed * valid_pixels[None, :], axis=1),
        ],
        axis=-1,
    )
    labels = labels.reshape(owners, MOST, 2)
    packed = jnp.einsum(
        "sf,fjc->sjc", placer, sar_faces, preferred_element_type=jnp.float32
    ).astype(jnp.bfloat16)
    arrived, recv_labels = (
        lax.all_to_all(
            packed.reshape(owners, MOST, length, channels_in),
            "tile",
            split_axis=0,
            concat_axis=0,
            tiled=True,
        ),
        lax.all_to_all(labels, "tile", split_axis=0, concat_axis=0, tiled=True),
    )
    raw_slots = arrived.reshape(slot_total, length, channels_in)
    received, saved = encoder_forward(raw_slots, encoder_first, encoder_second)
    recv_labels = recv_labels.reshape(slot_total, 2)
    recv_slot = recv_labels[:, 0]
    recv_count = recv_labels[:, 1]
    validity = (jnp.arange(length, dtype=jnp.int32)[None, :] < recv_count[:, None]).astype(
        jnp.float32
    )
    selector = recv_slot[:, None] == jnp.arange(tile_faces, dtype=jnp.int32)[None, :]
    masked = received * validity[..., None].astype(jnp.bfloat16)
    summed = jnp.einsum(
        "sp,sjc->pjc", selector.astype(jnp.bfloat16), masked, preferred_element_type=jnp.float32
    )
    covered = jnp.einsum(
        "sp,sj->pj", selector.astype(jnp.float32), validity, precision=highest
    ).reshape(-1, 1)
    condition = summed.reshape(-1, channels) / (1.0 + covered)
    time_value = (time_index[0].astype(jnp.float32) + 0.5) / NSTEPS
    noise_flat = noise_latent.astype(jnp.float32).reshape(-1, channels)
    clean_flat = clean_latent.astype(jnp.float32).reshape(-1, channels)
    hsum = (1.0 - time_value) * noise_flat + time_value * clean_flat + condition
    inverse = lax.rsqrt(jnp.mean(hsum * hsum, axis=-1, keepdims=True) + epsilon)
    normed = hsum * inverse
    lifted = normed * norm_gain
    activated = jax.nn.silu(lifted).astype(jnp.bfloat16).reshape(rows, columns, channels)
    extended = with_halo(activated, (("tile", 0),), 1)
    padded = jnp.pad(extended, ((0, 0), (1, 1), (0, 0)))
    predicted = convolve_forward(padded, conv_kernel, rows, columns)
    pixel_weight = (1 + cloud_mask).astype(jnp.float32).reshape(-1, 1)
    grad_pred = (pixel_weight * (predicted - clean_flat + noise_flat) / (rows * columns)).astype(
        jnp.bfloat16
    )
    grad_rows = with_halo(grad_pred.reshape(rows, columns, channels), (("tile", 0),), 1)
    padded_grad = jnp.pad(grad_rows, ((0, 0), (1, 1), (0, 0)))
    flows, kernel_part = convolve_backward(padded, padded_grad, conv_kernel, rows, columns)
    gain_part, grad_hsum = norm_backward(flows, lifted, normed, inverse, norm_gain)
    scaled = (grad_hsum / (1.0 + covered)).reshape(tile_faces, length, channels)
    slot_grads = (jnp.take(scaled, recv_slot, axis=0) * validity[..., None]).astype(jnp.bfloat16)
    first_part, second_part = encoder_backward(saved, slot_grads, encoder_first, encoder_second)
    reduced = lax.psum((kernel_part, gain_part, first_part, second_part), "tile")
    return (reduced[0], reduced[1], reduced[2], reduced[3])


def solution(mesh):
    placed = (
        P(("groups", "tile"), None, None),
        P(("groups", "tile"), None),
        P(("groups", "tile")),
        P(("groups", "tile")),
        P(("groups", "tile"), None),
        P(("groups", "tile")),
        P(("groups", "tile"), None, None),
        P(("groups", "tile"), None, None),
        P(),
        P(),
        P(),
        P(),
    )
    return jax.shard_map(
        body16 if mesh.shape["tile"] == 16 else body,
        mesh=mesh,
        in_specs=placed,
        out_specs=(
            P("groups", None, None),
            P("groups"),
            P("groups", None, None, None),
            P("groups", None, None, None),
        ),
        check_vma=False,
    )
```

```python
import jax
import jax.numpy as jnp
from jax import lax
from jax.experimental import pallas as pl
from jax.experimental.pallas import tpu as pltpu
from jax.sharding import PartitionSpec as P

MOST = 2
NSTEPS = 1000


highest = lax.Precision.HIGHEST
epsilon = 1e-06


def with_halo(block, sides, width):
    for axis, dim in sides:
        count = lax.axis_size(axis)
        forward = [(i, i + 1) for i in range(count - 1)]
        backward = [(target, source) for source, target in forward]
        low = lax.ppermute(
            lax.slice_in_dim(block, block.shape[dim] - width, None, axis=dim), axis, forward
        )
        high = lax.ppermute(lax.slice_in_dim(block, 0, width, axis=dim), axis, backward)
        block = jnp.concatenate([low, block, high], axis=dim)
    return block


def shift_line(values, offset):
    if offset == 0:
        return values
    zeros = jnp.zeros_like(values[:, : abs(offset)])
    if offset > 0:
        return jnp.concatenate([values[:, offset:], zeros], axis=1)
    return jnp.concatenate([zeros, values[:, :offset]], axis=1)


def taps_forward(inputs, weight, spread):
    summed = jnp.zeros(inputs.shape[:3] + (weight.shape[-1],), jnp.float32)
    for shift_tap in range(3):
        shifted = shift_line(inputs, (shift_tap - 1) * spread)
        summed = summed + jnp.einsum(
            "flgi,gio->flgo", shifted, weight[shift_tap], preferred_element_type=jnp.float32
        )
    return summed


def taps_weight_grad(inputs, cotangent, spread, exact):
    pieces = []
    for shift_tap in range(3):
        shifted = shift_line(inputs, (shift_tap - 1) * spread)
        if exact:
            pieces.append(
                jnp.einsum(
                    "flgi,flgo->gio", shifted.astype(jnp.float32), cotangent, precision=highest
                )
            )
        else:
            pieces.append(
                jnp.einsum("flgi,flgo->gio", shifted, cotangent, preferred_element_type=jnp.float32)
            )
    return jnp.stack(pieces)


def taps_input_grad(cotangent, weight, spread):
    summed = jnp.zeros(cotangent.shape[:3] + (weight.shape[2],), jnp.float32)
    for shift_tap in range(3):
        moved = jnp.einsum(
            "flgo,gio->flgi", cotangent, weight[shift_tap], preferred_element_type=jnp.float32
        )
        summed = summed + shift_line(moved, -(shift_tap - 1) * spread)
    return summed


def encoder_forward(sar_faces, first_w, second_w):
    face_count, length, channels_in = sar_faces.shape
    groups = first_w.shape[1]
    inputs = sar_faces.reshape(face_count, length, groups, -1)
    first_out = taps_forward(inputs, first_w, 1)
    hidden = jax.nn.silu(first_out).astype(jnp.bfloat16)
    second = taps_forward(hidden, second_w, 2)
    encoded = (
        (hidden.astype(jnp.float32) + second).reshape(face_count, length, -1).astype(jnp.bfloat16)
    )
    return (encoded, (inputs, first_out, hidden))


def encoder_backward(saved, grad_face, first_w, second_w):
    inputs, first_out, hidden = saved
    groups = first_w.shape[1]
    face_count, length, channels = grad_face.shape
    cotangent = grad_face.reshape(face_count, length, groups, -1)
    second_part = taps_weight_grad(hidden, cotangent, 2, False)
    grad_hidden = cotangent.astype(jnp.float32) + taps_input_grad(cotangent, second_w, 2)
    logistic = jax.nn.sigmoid(first_out)
    grad_first_out = grad_hidden * logistic * (1.0 + first_out * (1.0 - logistic))
    first_part = taps_weight_grad(inputs, grad_first_out, 1, True)
    return (first_part, second_part)


def convolve_forward(padded, kernel, rows, columns):
    channels = kernel.shape[-1]
    summed = jnp.zeros((rows * columns, channels), jnp.float32)
    for row_tap in range(3):
        for col_tap in range(3):
            window = padded[row_tap : row_tap + rows, col_tap : col_tap + columns].reshape(
                -1, channels
            )
            summed = summed + jnp.dot(
                window, kernel[3 * row_tap + col_tap], preferred_element_type=jnp.float32
            )
    return summed


def convolve_backward(padded_act, padded_grad, kernel, rows, columns):
    channels = kernel.shape[-1]
    incoming = padded_grad[1 : rows + 1, 1 : columns + 1].reshape(-1, channels)
    flows = jnp.zeros((rows * columns, channels), jnp.float32)
    kernels = []
    for row_tap in range(3):
        for col_tap in range(3):
            window = padded_act[row_tap : row_tap + rows, col_tap : col_tap + columns].reshape(
                -1, channels
            )
            kernels.append(
                lax.dot_general(
                    window, incoming, (((0,), (0,)), ((), ())), preferred_element_type=jnp.float32
                )
            )
            moved = padded_grad[
                2 - row_tap : 2 - row_tap + rows, 2 - col_tap : 2 - col_tap + columns
            ].reshape(-1, channels)
            flows = flows + lax.dot_general(
                moved,
                kernel[3 * row_tap + col_tap],
                (((1,), (1,)), ((), ())),
                preferred_element_type=jnp.float32,
            )
    return (flows, jnp.stack(kernels))


def norm_backward(flows, lifted, normed, inverse, gain):
    logistic = jax.nn.sigmoid(lifted)
    grad_lift = flows * logistic * (1.0 + lifted * (1.0 - logistic))
    gain_part = jnp.sum(grad_lift * normed, axis=0)
    grad_norm = grad_lift * gain
    grad_hsum = inverse * (
        grad_norm - normed * jnp.mean(grad_norm * normed, axis=-1, keepdims=True)
    )
    return (gain_part, grad_hsum)


MESH = pl.DeviceIdType.MESH
VM = pltpu.VMEM


def entry_barrier(me, count):
    barrier = pltpu.get_barrier_semaphore()
    for k in range(1, count):
        pl.semaphore_signal(
            barrier, inc=1, device_id={"tile": lax.rem(me + k, count)}, device_id_type=MESH
        )
    pl.semaphore_wait(barrier, count - 1)


def exchange_kernel(count, x_ref, o_ref, send, recv, local):
    me = lax.axis_index("tile")
    entry_barrier(me, count)
    own = pltpu.make_async_copy(x_ref.at[me], o_ref.at[me], local)
    own.start()
    copies = []
    for k in range(1, count):
        to = lax.rem(me + k, count)
        copy = pltpu.make_async_remote_copy(
            src_ref=x_ref.at[to],
            dst_ref=o_ref.at[me],
            send_sem=send.at[k - 1],
            recv_sem=recv.at[k - 1],
            device_id={"tile": to},
            device_id_type=MESH,
        )
        copy.start()
        copies.append(copy)
    own.wait()
    for copy in copies:
        copy.wait()


def exchange(packed):
    count = packed.shape[0]
    return pl.pallas_call(
        lambda *refs: exchange_kernel(count, *refs),
        out_shape=jax.ShapeDtypeStruct(packed.shape, packed.dtype),
        in_specs=[pl.BlockSpec(memory_space=VM)],
        out_specs=pl.BlockSpec(memory_space=VM),
        scratch_shapes=[
            pltpu.SemaphoreType.DMA((count - 1,)),
            pltpu.SemaphoreType.DMA((count - 1,)),
            pltpu.SemaphoreType.DMA,
        ],
        compiler_params=pltpu.CompilerParams(collective_id=0, has_side_effects=True),
        name="exchange",
    )(packed)


class Gather:
    def __init__(self, buf, send, recv):
        self.buf, self.send_sem, self.recv_sem = buf, send, recv
        self.me = lax.axis_index("tile")
        self.core = lax.rem(self.me, 2)
        self.x = lax.rem(self.me // 2, 2)
        self.z = self.me // 4
        self.x_peer = self.z * 4 + (1 - self.x) * 2 + self.core
        self.sibling = self.z * 4 + self.x * 2 + (1 - self.core)

    def copy(self, chunk, to, index):
        return pltpu.make_async_remote_copy(
            src_ref=self.buf.at[chunk],
            dst_ref=self.buf.at[chunk],
            send_sem=self.send_sem.at[index],
            recv_sem=self.recv_sem.at[chunk],
            device_id={"tile": to},
            device_id_type=MESH,
        )

    def at(self, back, x, core):
        return lax.rem(self.z + 4 - back, 4) * 4 + x * 2 + core

    def start(self):
        self.copy(self.me, self.x_peer, 3).start()
        self.copy(self.me, self.sibling, 4).start()
        for k in (1, 3, 2):
            to = lax.rem(self.z + k, 4) * 4 + self.x * 2 + self.core
            self.copy(self.me, to, k - 1).start()

    def pass_z(self, back):
        chunk = self.at(back, self.x, self.core)
        self.copy(chunk, self.x_peer, 0).wait_recv()
        self.copy(chunk, self.x_peer, 5 + 2 * (back - 1)).start()
        self.copy(chunk, self.sibling, 6 + 2 * (back - 1)).start()

    def pass_x(self, back):
        chunk = self.at(back, 1 - self.x, self.core)
        self.copy(chunk, self.sibling, 0).wait_recv()
        self.copy(chunk, self.sibling, 11 + back).start()

    def take(self, back):
        for x in (self.x, 1 - self.x):
            chunk = self.at(back, x, 1 - self.core)
            self.copy(chunk, self.sibling, 0).wait_recv()

    def drain(self):
        for index in range(15):
            self.copy(self.me, self.sibling, index).wait_send()


def moved(values, offset, axis):
    extent = values.shape[axis]
    rolled = pltpu.roll(values, (-offset) % extent, axis)
    place = lax.broadcasted_iota(jnp.int32, values.shape, axis)
    return jnp.where(place == (extent - 1 if offset > 0 else 0), 0.0, rolled)


def halo_copies(src, halo, send, recv, me):
    up = pltpu.make_async_remote_copy(
        src_ref=src,
        dst_ref=halo.at[1],
        send_sem=send.at[0],
        recv_sem=recv.at[1],
        device_id={"tile": jnp.maximum(me - 1, 0)},
        device_id_type=MESH,
    )
    down = pltpu.make_async_remote_copy(
        src_ref=src,
        dst_ref=halo.at[0],
        send_sem=send.at[1],
        recv_sem=recv.at[0],
        device_id={"tile": jnp.minimum(me + 1, 15)},
        device_id_type=MESH,
    )
    return up, down


def middle_kernel(
    act_ref,
    clean_ref,
    noise_ref,
    weight_ref,
    kernel_ref,
    flows_ref,
    grad_ref,
    gathered_ref,
    halo_a,
    halo_g,
    gather_send,
    gather_recv,
    a_send,
    a_recv,
    g_send,
    g_recv,
):
    me = lax.axis_index("tile")
    last = 15
    columns = act_ref.shape[0]
    f32 = jnp.float32
    entry_barrier(me, 16)
    a_up, a_down = halo_copies(act_ref, halo_a, a_send, a_recv, me)
    g_up, g_down = halo_copies(grad_ref, halo_g, g_send, g_recv, me)

    @pl.when(me > 0)
    def _():
        a_up.start()

    @pl.when(me < last)
    def _():
        a_down.start()

    gathered_ref[me] = act_ref[...].T
    gather = Gather(gathered_ref, gather_send, gather_recv)
    gather.start()

    @pl.when(me == 0)
    def _():
        halo_a[0] = jnp.zeros_like(halo_a[0])
        halo_g[0] = jnp.zeros_like(halo_g[0])

    @pl.when(me == last)
    def _():
        halo_a[1] = jnp.zeros_like(halo_a[1])
        halo_g[1] = jnp.zeros_like(halo_g[1])

    own = act_ref[...]
    sums = [jnp.dot(own, kernel_ref[3 + d], preferred_element_type=f32) for d in range(3)]

    @pl.when(me > 0)
    def _():
        a_down.wait_recv()

    @pl.when(me < last)
    def _():
        a_up.wait_recv()

    above, below = halo_a[0], halo_a[1]
    sums = [
        sums[d]
        + jnp.dot(above, kernel_ref[d], preferred_element_type=f32)
        + jnp.dot(below, kernel_ref[6 + d], preferred_element_type=f32)
        for d in range(3)
    ]
    predicted = sums[1] + moved(sums[0], -1, 0) + moved(sums[2], 1, 0)
    grad = (
        weight_ref[...]
        * (predicted - clean_ref[...].astype(f32) + noise_ref[...].astype(f32))
        / columns
    ).astype(jnp.bfloat16)
    grad_ref[...] = grad

    @pl.when(me > 0)
    def _():
        g_up.start()

    @pl.when(me < last)
    def _():
        g_down.start()

    def back(values, tap):
        return lax.dot_general(
            values, kernel_ref[tap], (((1,), (1,)), ((), ())), preferred_element_type=f32
        )

    sums = [back(grad, 3 + d) for d in range(3)]
    for k in (1, 3, 2):
        gather.pass_z(k)

    @pl.when(me > 0)
    def _():
        g_down.wait_recv()

    @pl.when(me < last)
    def _():
        g_up.wait_recv()

    above, below = halo_g[0], halo_g[1]
    sums = [sums[d] + back(below, d) + back(above, 6 + d) for d in range(3)]
    flows_ref[...] = sums[1] + moved(sums[0], 1, 0) + moved(sums[2], -1, 0)
    for k in (0, 1, 3, 2):
        gather.pass_x(k)
    for k in (0, 1, 3, 2):
        gather.take(k)
    gather.drain()

    @pl.when(me > 0)
    def _():
        a_up.wait_send()
        g_up.wait_send()

    @pl.when(me < last)
    def _():
        a_down.wait_send()
        g_down.wait_send()


def middle(activated, clean, noise, pixel_weight, kernel):
    pixels, channels = activated.shape
    dma = pltpu.SemaphoreType.DMA
    return pl.pallas_call(
        middle_kernel,
        out_shape=(
            jax.ShapeDtypeStruct((pixels, channels), jnp.float32),
            jax.ShapeDtypeStruct((pixels, channels), jnp.bfloat16),
            jax.ShapeDtypeStruct((16, channels, pixels), jnp.bfloat16),
        ),
        in_specs=[pl.BlockSpec(memory_space=VM)] * 5,
        out_specs=(pl.BlockSpec(memory_space=VM),) * 3,
        scratch_shapes=[
            VM((2, pixels, channels), jnp.bfloat16),
            VM((2, pixels, channels), jnp.bfloat16),
            dma((15,)),
            dma((16,)),
            dma((2,)),
            dma((2,)),
            dma((2,)),
            dma((2,)),
        ],
        compiler_params=pltpu.CompilerParams(
            collective_id=1, has_side_effects=True, vmem_limit_bytes=40 * 2**20
        ),
        name="middle",
    )(activated, clean, noise, pixel_weight, kernel)


def outer_kernel(
    grad_ref,
    gathered_ref,
    parts_ref,
    result_ref,
    total_ref,
    grads,
    shifted,
    sums,
    landed,
    gather_send,
    gather_recv,
    half_send,
    half_recv,
    sum_send,
    sum_recv,
):
    me = lax.axis_index("tile")
    channels, pixels = gathered_ref.shape[1:]
    part = channels // 2
    f32 = jnp.float32
    entry_barrier(me, 16)
    grads[me] = grad_ref[...]
    gather = Gather(grads, gather_send, gather_recv)
    gather.start()
    core, z = gather.core, gather.z
    mine = pl.ds(pl.multiple_of(core * part, part), part)
    rows = parts_ref.shape[0] // 2
    my_rows = pl.ds(pl.multiple_of(core * rows, 8), rows)
    other_rows = pl.ds(pl.multiple_of((1 - core) * rows, 8), rows)
    z_near = (z + 1 - 2 * lax.rem(z, 2)) * 4 + lax.rem(me, 4)
    z_far = lax.rem(z + 2, 4) * 4 + lax.rem(me, 4)

    def sum_copy(src, dst, stage, to):
        return pltpu.make_async_remote_copy(
            src_ref=src,
            dst_ref=dst,
            send_sem=sum_send.at[stage],
            recv_sem=sum_recv.at[stage],
            device_id={"tile": to},
            device_id_type=MESH,
        )

    hops = [
        sum_copy(parts_ref.at[other_rows], landed.at[0], 0, gather.sibling),
        sum_copy(sums.at[0], landed.at[1], 1, gather.x_peer),
        sum_copy(sums.at[1], landed.at[2], 2, z_near),
        sum_copy(sums.at[2], landed.at[3], 3, z_far),
        sum_copy(total_ref.at[my_rows], total_ref.at[my_rows], 4, gather.sibling),
    ]
    hops[0].start()

    def add_hop(stage):
        hops[stage].wait_recv()
        held = parts_ref[my_rows, :] if stage == 0 else sums[stage - 1]
        if stage < 3:
            sums[stage] = held + landed[stage]
        else:
            total_ref[my_rows, :] = held + landed[stage]
        hops[stage + 1].start()

    zeros = jnp.zeros((3 * part, pixels), jnp.bfloat16)
    shifted[:, 0:pixels] = zeros
    shifted[:, 17 * pixels : 18 * pixels] = zeros

    def shift_some(low, high):
        def step(chunk, carry):
            plain = gathered_ref[chunk, mine, :]
            wide = plain.astype(f32)
            here = pl.ds(pl.multiple_of((chunk + 1) * pixels, pixels), pixels)
            shifted[0:part, here] = moved(wide, -1, 1).astype(jnp.bfloat16)
            shifted[part : 2 * part, here] = plain
            shifted[2 * part : 3 * part, here] = moved(wide, 1, 1).astype(jnp.bfloat16)
            return carry

        lax.fori_loop(low, high, step, 0)

    def half_copy(row):
        return pltpu.make_async_remote_copy(
            src_ref=result_ref.at[pl.ds(3 * row, 3), mine],
            dst_ref=result_ref.at[pl.ds(3 * row, 3), mine],
            send_sem=half_send.at[row],
            recv_sem=half_recv.at[row],
            device_id={"tile": gather.sibling},
            device_id_type=MESH,
        )

    def multiply(back, order):
        base = lax.rem(z + 4 - back, 4) * 4
        right = grads[pl.ds(base, 4)].reshape(4 * pixels, channels)

        def step(row, carry):
            start = pl.multiple_of((base + row) * pixels, pixels)
            left = shifted[:, pl.ds(start, 4 * pixels)]
            product = jnp.dot(left, right, preferred_element_type=f32)
            for d in range(3):
                piece = product[d * part : (d + 1) * part]
                if order == 0:
                    result_ref[3 * row + d, mine, :] = piece
                else:
                    result_ref[3 * row + d, mine, :] = result_ref[3 * row + d, mine, :] + piece
            if order == 3:
                half_copy(row).start()
            return carry

        lax.fori_loop(0, 3, step, 0)

    shift_some(0, 6)
    gather.pass_x(0)
    gather.pass_z(1)
    add_hop(0)
    shift_some(6, 11)
    gather.pass_z(3)
    shift_some(11, 16)
    gather.pass_z(2)
    add_hop(1)
    gather.take(0)
    multiply(0, 0)
    for order, k in ((1, 1), (2, 3), (3, 2)):
        gather.pass_x(k)
        gather.take(k)
        if order < 3:
            add_hop(order + 1)
        multiply(k, order)
    hops[4].wait_recv()
    gather.drain()
    for hop in hops:
        hop.wait_send()
    for row in range(3):
        half_copy(row).wait()


def outer(grad, gathered, parts):
    pixels, channels = grad.shape
    rows = parts.shape[0] // 2
    dma = pltpu.SemaphoreType.DMA
    return pl.pallas_call(
        outer_kernel,
        out_shape=(
            jax.ShapeDtypeStruct((9, channels, channels), jnp.float32),
            jax.ShapeDtypeStruct(parts.shape, jnp.float32),
        ),
        in_specs=[pl.BlockSpec(memory_space=VM)] * 3,
        out_specs=(pl.BlockSpec(memory_space=VM),) * 2,
        scratch_shapes=[
            VM((16, pixels, channels), jnp.bfloat16),
            VM((3 * channels // 2, 18 * pixels), jnp.bfloat16),
            VM((3, rows, 128), jnp.float32),
            VM((4, rows, 128), jnp.float32),
            dma((15,)),
            dma((16,)),
            dma((3,)),
            dma((3,)),
            dma((5,)),
            dma((5,)),
        ],
        compiler_params=pltpu.CompilerParams(
            collective_id=2, has_side_effects=True, vmem_limit_bytes=48 * 2**20
        ),
        name="outer",
    )(grad, gathered, parts)


def body16(
    sar_faces,
    dest_owner,
    face_slot,
    valid_pixels,
    cloud_mask,
    time_index,
    clean_latent,
    noise_latent,
    encoder_first,
    encoder_second,
    conv_kernel,
    norm_gain,
):
    owners = lax.axis_size("tile")
    slot_total = owners * MOST
    face_count, length, channels_in = sar_faces.shape
    rows, columns, channels = clean_latent.shape
    tile_faces = rows * columns // length
    owner_list = dest_owner[:, 0]
    onehot = (owner_list[:, None] == jnp.arange(owners, dtype=jnp.int32)[None, :]).astype(jnp.int32)
    before = jnp.cumsum(onehot, axis=0) - onehot
    within = jnp.sum(before * onehot, axis=1)
    buffer_at = owner_list * MOST + within
    placed = (jnp.arange(slot_total, dtype=jnp.int32)[:, None] == buffer_at[None, :]).astype(
        jnp.int32
    )
    placer = placed.astype(jnp.bfloat16)
    labels = jnp.stack(
        [
            jnp.sum(placed * face_slot[None, :], axis=1),
            jnp.sum(placed * valid_pixels[None, :], axis=1),
        ],
        axis=-1,
    )
    packed = jnp.einsum(
        "sf,fjc->sjc", placer, sar_faces, preferred_element_type=jnp.float32
    ).astype(jnp.bfloat16)
    label_rows = jnp.pad(
        labels.astype(jnp.bfloat16)[:, None, :],
        ((0, 0), (0, length - 1), (0, channels_in - 2)),
    )
    arrived = exchange(
        jnp.concatenate([packed, label_rows], axis=1).reshape(
            owners, MOST * 2 * length, channels_in
        )
    ).reshape(slot_total, 2 * length, channels_in)
    raw_slots = arrived[:, :length]
    recv_labels = arrived[:, length, :2].astype(jnp.int32)
    received, saved = encoder_forward(raw_slots, encoder_first, encoder_second)
    recv_slot = recv_labels[:, 0]
    recv_count = recv_labels[:, 1]
    validity = (jnp.arange(length, dtype=jnp.int32)[None, :] < recv_count[:, None]).astype(
        jnp.float32
    )
    selector = recv_slot[:, None] == jnp.arange(tile_faces, dtype=jnp.int32)[None, :]
    masked = received * validity[..., None].astype(jnp.bfloat16)
    summed = jnp.einsum(
        "sp,sjc->pjc", selector.astype(jnp.bfloat16), masked, preferred_element_type=jnp.float32
    )
    covered = jnp.einsum(
        "sp,sj->pj", selector.astype(jnp.float32), validity, precision=highest
    ).reshape(-1, 1)
    condition = summed.reshape(-1, channels) / (1.0 + covered)
    time_value = (time_index[0].astype(jnp.float32) + 0.5) / NSTEPS
    noise_flat = noise_latent.astype(jnp.float32).reshape(-1, channels)
    clean_flat = clean_latent.astype(jnp.float32).reshape(-1, channels)
    hsum = (1.0 - time_value) * noise_flat + time_value * clean_flat + condition
    inverse = lax.rsqrt(jnp.mean(hsum * hsum, axis=-1, keepdims=True) + epsilon)
    normed = hsum * inverse
    lifted = normed * norm_gain
    activated = jax.nn.silu(lifted).astype(jnp.bfloat16)
    pixel_weight = (1 + cloud_mask).astype(jnp.float32).reshape(-1, 1)
    flows, grad_pred, gathered = middle(
        activated,
        clean_latent.reshape(-1, channels),
        noise_latent.reshape(-1, channels),
        pixel_weight,
        conv_kernel,
    )
    gain_part, grad_hsum = norm_backward(flows, lifted, normed, inverse, norm_gain)
    scaled = (grad_hsum / (1.0 + covered)).reshape(tile_faces, length, channels)
    slot_grads = (jnp.take(scaled, recv_slot, axis=0) * validity[..., None]).astype(jnp.bfloat16)
    first_part, second_part = encoder_backward(saved, slot_grads, encoder_first, encoder_second)
    parts = (second_part, first_part, gain_part)
    flat = jnp.concatenate([part.reshape(-1, 128) for part in parts], axis=0)
    flat = jnp.pad(flat, ((0, -flat.shape[0] % 16), (0, 0)))
    grad_kernel, total = outer(grad_pred, gathered, flat)
    sums = []
    at = 0
    for part in parts:
        count = part.size // 128
        sums.append(total[at : at + count].reshape(part.shape))
        at += count
    return (grad_kernel, sums[2], sums[1], sums[0])


def body(
    sar_faces,
    dest_owner,
    face_slot,
    valid_pixels,
    cloud_mask,
    time_index,
    clean_latent,
    noise_latent,
    encoder_first,
    encoder_second,
    conv_kernel,
    norm_gain,
):
    owners = lax.axis_size("tile")
    slot_total = owners * MOST
    face_count, length, channels_in = sar_faces.shape
    rows, columns, channels = clean_latent.shape
    tile_faces = rows * columns // length
    owner_list = dest_owner[:, 0]
    onehot = (owner_list[:, None] == jnp.arange(owners, dtype=jnp.int32)[None, :]).astype(jnp.int32)
    before = jnp.cumsum(onehot, axis=0) - onehot
    within = jnp.sum(before * onehot, axis=1)
    buffer_at = owner_list * MOST + within
    placed = (jnp.arange(slot_total, dtype=jnp.int32)[:, None] == buffer_at[None, :]).astype(
        jnp.int32
    )
    placer = placed.astype(jnp.bfloat16)
    labels = jnp.stack(
        [
            jnp.sum(placed * face_slot[None, :], axis=1),
            jnp.sum(placed * valid_pixels[None, :], axis=1),
        ],
        axis=-1,
    )
    labels = labels.reshape(owners, MOST, 2)
    packed = jnp.einsum(
        "sf,fjc->sjc", placer, sar_faces, preferred_element_type=jnp.float32
    ).astype(jnp.bfloat16)
    arrived, recv_labels = (
        lax.all_to_all(
            packed.reshape(owners, MOST, length, channels_in),
            "tile",
            split_axis=0,
            concat_axis=0,
            tiled=True,
        ),
        lax.all_to_all(labels, "tile", split_axis=0, concat_axis=0, tiled=True),
    )
    raw_slots = arrived.reshape(slot_total, length, channels_in)
    received, saved = encoder_forward(raw_slots, encoder_first, encoder_second)
    recv_labels = recv_labels.reshape(slot_total, 2)
    recv_slot = recv_labels[:, 0]
    recv_count = recv_labels[:, 1]
    validity = (jnp.arange(length, dtype=jnp.int32)[None, :] < recv_count[:, None]).astype(
        jnp.float32
    )
    selector = recv_slot[:, None] == jnp.arange(tile_faces, dtype=jnp.int32)[None, :]
    masked = received * validity[..., None].astype(jnp.bfloat16)
    summed = jnp.einsum(
        "sp,sjc->pjc", selector.astype(jnp.bfloat16), masked, preferred_element_type=jnp.float32
    )
    covered = jnp.einsum(
        "sp,sj->pj", selector.astype(jnp.float32), validity, precision=highest
    ).reshape(-1, 1)
    condition = summed.reshape(-1, channels) / (1.0 + covered)
    time_value = (time_index[0].astype(jnp.float32) + 0.5) / NSTEPS
    noise_flat = noise_latent.astype(jnp.float32).reshape(-1, channels)
    clean_flat = clean_latent.astype(jnp.float32).reshape(-1, channels)
    hsum = (1.0 - time_value) * noise_flat + time_value * clean_flat + condition
    inverse = lax.rsqrt(jnp.mean(hsum * hsum, axis=-1, keepdims=True) + epsilon)
    normed = hsum * inverse
    lifted = normed * norm_gain
    activated = jax.nn.silu(lifted).astype(jnp.bfloat16).reshape(rows, columns, channels)
    extended = with_halo(activated, (("tile", 0),), 1)
    padded = jnp.pad(extended, ((0, 0), (1, 1), (0, 0)))
    predicted = convolve_forward(padded, conv_kernel, rows, columns)
    pixel_weight = (1 + cloud_mask).astype(jnp.float32).reshape(-1, 1)
    grad_pred = (pixel_weight * (predicted - clean_flat + noise_flat) / (rows * columns)).astype(
        jnp.bfloat16
    )
    grad_rows = with_halo(grad_pred.reshape(rows, columns, channels), (("tile", 0),), 1)
    padded_grad = jnp.pad(grad_rows, ((0, 0), (1, 1), (0, 0)))
    flows, kernel_part = convolve_backward(padded, padded_grad, conv_kernel, rows, columns)
    gain_part, grad_hsum = norm_backward(flows, lifted, normed, inverse, norm_gain)
    scaled = (grad_hsum / (1.0 + covered)).reshape(tile_faces, length, channels)
    slot_grads = (jnp.take(scaled, recv_slot, axis=0) * validity[..., None]).astype(jnp.bfloat16)
    first_part, second_part = encoder_backward(saved, slot_grads, encoder_first, encoder_second)
    reduced = lax.psum((kernel_part, gain_part, first_part, second_part), "tile")
    return (reduced[0], reduced[1], reduced[2], reduced[3])


def solution(mesh):
    placed = (
        P(("groups", "tile"), None, None),
        P(("groups", "tile"), None),
        P(("groups", "tile")),
        P(("groups", "tile")),
        P(("groups", "tile"), None),
        P(("groups", "tile")),
        P(("groups", "tile"), None, None),
        P(("groups", "tile"), None, None),
        P(),
        P(),
        P(),
        P(),
    )
    return jax.shard_map(
        body16 if mesh.shape["tile"] == 16 else body,
        mesh=mesh,
        in_specs=placed,
        out_specs=(
            P("groups", None, None),
            P("groups"),
            P("groups", None, None, None),
            P("groups", None, None, None),
        ),
        check_vma=False,
    )
```

```python
import jax
import jax.numpy as jnp
from jax import lax
from jax.experimental import pallas as pl
from jax.experimental.pallas import tpu as pltpu
from jax.sharding import PartitionSpec as P

MOST = 2
NSTEPS = 1000


highest = lax.Precision.HIGHEST
epsilon = 1e-06


def with_halo(block, sides, width):
    for axis, dim in sides:
        count = lax.axis_size(axis)
        forward = [(i, i + 1) for i in range(count - 1)]
        backward = [(target, source) for source, target in forward]
        low = lax.ppermute(
            lax.slice_in_dim(block, block.shape[dim] - width, None, axis=dim), axis, forward
        )
        high = lax.ppermute(lax.slice_in_dim(block, 0, width, axis=dim), axis, backward)
        block = jnp.concatenate([low, block, high], axis=dim)
    return block


def shift_line(values, offset):
    if offset == 0:
        return values
    zeros = jnp.zeros_like(values[:, : abs(offset)])
    if offset > 0:
        return jnp.concatenate([values[:, offset:], zeros], axis=1)
    return jnp.concatenate([zeros, values[:, :offset]], axis=1)


def taps_forward(inputs, weight, spread):
    summed = jnp.zeros(inputs.shape[:3] + (weight.shape[-1],), jnp.float32)
    for shift_tap in range(3):
        shifted = shift_line(inputs, (shift_tap - 1) * spread)
        summed = summed + jnp.einsum(
            "flgi,gio->flgo", shifted, weight[shift_tap], preferred_element_type=jnp.float32
        )
    return summed


def taps_weight_grad(inputs, cotangent, spread, exact):
    pieces = []
    for shift_tap in range(3):
        shifted = shift_line(inputs, (shift_tap - 1) * spread)
        if exact:
            pieces.append(
                jnp.einsum(
                    "flgi,flgo->gio", shifted.astype(jnp.float32), cotangent, precision=highest
                )
            )
        else:
            pieces.append(
                jnp.einsum("flgi,flgo->gio", shifted, cotangent, preferred_element_type=jnp.float32)
            )
    return jnp.stack(pieces)


def taps_input_grad(cotangent, weight, spread):
    summed = jnp.zeros(cotangent.shape[:3] + (weight.shape[2],), jnp.float32)
    for shift_tap in range(3):
        moved = jnp.einsum(
            "flgo,gio->flgi", cotangent, weight[shift_tap], preferred_element_type=jnp.float32
        )
        summed = summed + shift_line(moved, -(shift_tap - 1) * spread)
    return summed


def encoder_forward(sar_faces, first_w, second_w):
    face_count, length, channels_in = sar_faces.shape
    groups = first_w.shape[1]
    inputs = sar_faces.reshape(face_count, length, groups, -1)
    first_out = taps_forward(inputs, first_w, 1)
    hidden = jax.nn.silu(first_out).astype(jnp.bfloat16)
    second = taps_forward(hidden, second_w, 2)
    encoded = (
        (hidden.astype(jnp.float32) + second).reshape(face_count, length, -1).astype(jnp.bfloat16)
    )
    return (encoded, (inputs, first_out, hidden))


def encoder_backward(saved, grad_face, first_w, second_w):
    inputs, first_out, hidden = saved
    groups = first_w.shape[1]
    face_count, length, channels = grad_face.shape
    cotangent = grad_face.reshape(face_count, length, groups, -1)
    second_part = taps_weight_grad(hidden, cotangent, 2, False)
    grad_hidden = cotangent.astype(jnp.float32) + taps_input_grad(cotangent, second_w, 2)
    logistic = jax.nn.sigmoid(first_out)
    grad_first_out = grad_hidden * logistic * (1.0 + first_out * (1.0 - logistic))
    first_part = taps_weight_grad(inputs, grad_first_out, 1, True)
    return (first_part, second_part)


def convolve_forward(padded, kernel, rows, columns):
    channels = kernel.shape[-1]
    summed = jnp.zeros((rows * columns, channels), jnp.float32)
    for row_tap in range(3):
        for col_tap in range(3):
            window = padded[row_tap : row_tap + rows, col_tap : col_tap + columns].reshape(
                -1, channels
            )
            summed = summed + jnp.dot(
                window, kernel[3 * row_tap + col_tap], preferred_element_type=jnp.float32
            )
    return summed


def convolve_backward(padded_act, padded_grad, kernel, rows, columns):
    channels = kernel.shape[-1]
    incoming = padded_grad[1 : rows + 1, 1 : columns + 1].reshape(-1, channels)
    flows = jnp.zeros((rows * columns, channels), jnp.float32)
    kernels = []
    for row_tap in range(3):
        for col_tap in range(3):
            window = padded_act[row_tap : row_tap + rows, col_tap : col_tap + columns].reshape(
                -1, channels
            )
            kernels.append(
                lax.dot_general(
                    window, incoming, (((0,), (0,)), ((), ())), preferred_element_type=jnp.float32
                )
            )
            moved = padded_grad[
                2 - row_tap : 2 - row_tap + rows, 2 - col_tap : 2 - col_tap + columns
            ].reshape(-1, channels)
            flows = flows + lax.dot_general(
                moved,
                kernel[3 * row_tap + col_tap],
                (((1,), (1,)), ((), ())),
                preferred_element_type=jnp.float32,
            )
    return (flows, jnp.stack(kernels))


def norm_backward(flows, lifted, normed, inverse, gain):
    logistic = jax.nn.sigmoid(lifted)
    grad_lift = flows * logistic * (1.0 + lifted * (1.0 - logistic))
    gain_part = jnp.sum(grad_lift * normed, axis=0)
    grad_norm = grad_lift * gain
    grad_hsum = inverse * (
        grad_norm - normed * jnp.mean(grad_norm * normed, axis=-1, keepdims=True)
    )
    return (gain_part, grad_hsum)


MESH = pl.DeviceIdType.MESH
VM = pltpu.VMEM


def entry_barrier(me, count):
    barrier = pltpu.get_barrier_semaphore()
    for k in range(1, count):
        pl.semaphore_signal(
            barrier, inc=1, device_id={"tile": lax.rem(me + k, count)}, device_id_type=MESH
        )
    pl.semaphore_wait(barrier, count - 1)


def exchange_kernel(count, x_ref, o_ref, send, recv, local):
    me = lax.axis_index("tile")
    entry_barrier(me, count)
    own = pltpu.make_async_copy(x_ref.at[me], o_ref.at[me], local)
    own.start()
    copies = []
    for k in range(1, count):
        to = lax.rem(me + k, count)
        copy = pltpu.make_async_remote_copy(
            src_ref=x_ref.at[to],
            dst_ref=o_ref.at[me],
            send_sem=send.at[k - 1],
            recv_sem=recv.at[k - 1],
            device_id={"tile": to},
            device_id_type=MESH,
        )
        copy.start()
        copies.append(copy)
    own.wait()
    for copy in copies:
        copy.wait()


def exchange(packed):
    count = packed.shape[0]
    return pl.pallas_call(
        lambda *refs: exchange_kernel(count, *refs),
        out_shape=jax.ShapeDtypeStruct(packed.shape, packed.dtype),
        in_specs=[pl.BlockSpec(memory_space=VM)],
        out_specs=pl.BlockSpec(memory_space=VM),
        scratch_shapes=[
            pltpu.SemaphoreType.DMA((count - 1,)),
            pltpu.SemaphoreType.DMA((count - 1,)),
            pltpu.SemaphoreType.DMA,
        ],
        compiler_params=pltpu.CompilerParams(collective_id=0, has_side_effects=True),
        name="exchange",
    )(packed)


class Gather:
    def __init__(self, buf, send, recv):
        self.buf, self.send_sem, self.recv_sem = buf, send, recv
        self.me = lax.axis_index("tile")
        self.core = lax.rem(self.me, 2)
        self.x = lax.rem(self.me // 2, 2)
        self.z = z = self.me // 4
        self.x_peer = z * 4 + (1 - self.x) * 2 + self.core
        self.sibling = z * 4 + self.x * 2 + (1 - self.core)
        self.planes = [
            z,
            jnp.where(z == 0, 1, z - 1),
            jnp.where(z == 0, 2, jnp.where(z == 3, 1, z + 1)),
            jnp.where(z < 2, 3, 0),
        ]

    def copy(self, chunk, to, index):
        return pltpu.make_async_remote_copy(
            src_ref=self.buf.at[chunk],
            dst_ref=self.buf.at[chunk],
            send_sem=self.send_sem.at[index],
            recv_sem=self.recv_sem.at[chunk],
            device_id={"tile": to},
            device_id_type=MESH,
        )

    def at(self, step, x, core):
        return self.planes[step] * 4 + x * 2 + core

    def along(self, step):
        place = lax.rem(self.me, 4)
        onward = jnp.where(self.planes[step] < self.z, self.z + 1, self.z - 1)
        valid = (onward >= 0) & (onward <= 3)
        return jnp.clip(onward, 0, 3) * 4 + place, valid

    def start(self):
        place = lax.rem(self.me, 4)

        @pl.when(self.z < 3)
        def _():
            self.copy(self.me, jnp.minimum(self.z + 1, 3) * 4 + place, 0).start()

        @pl.when(self.z > 0)
        def _():
            self.copy(self.me, jnp.maximum(self.z - 1, 0) * 4 + place, 1).start()

        self.copy(self.me, self.x_peer, 2).start()
        self.copy(self.me, self.sibling, 3).start()

    def pass_z(self, step):
        chunk = self.at(step, self.x, self.core)
        self.copy(chunk, self.x_peer, 0).wait_recv()
        to, valid = self.along(step)

        @pl.when(valid)
        def _():
            self.copy(chunk, to, 3 + step).start()

        self.copy(chunk, self.x_peer, 6 + step).start()
        self.copy(chunk, self.sibling, 9 + step).start()

    def pass_x(self, step):
        chunk = self.at(step, 1 - self.x, self.core)
        self.copy(chunk, self.sibling, 0).wait_recv()
        self.copy(chunk, self.sibling, 13 + step).start()

    def take(self, step):
        for x in (self.x, 1 - self.x):
            chunk = self.at(step, x, 1 - self.core)
            self.copy(chunk, self.sibling, 0).wait_recv()

    def drain(self):
        @pl.when(self.z < 3)
        def _():
            self.copy(self.me, self.sibling, 0).wait_send()

        @pl.when(self.z > 0)
        def _():
            self.copy(self.me, self.sibling, 1).wait_send()

        for step in range(1, 4):
            _, valid = self.along(step)

            @pl.when(valid)
            def _():
                self.copy(self.me, self.sibling, 3 + step).wait_send()

        for index in (2, 3, 7, 8, 9, 10, 11, 12, 13, 14, 15, 16):
            self.copy(self.me, self.sibling, index).wait_send()


def moved(values, offset, axis):
    extent = values.shape[axis]
    rolled = pltpu.roll(values, (-offset) % extent, axis)
    place = lax.broadcasted_iota(jnp.int32, values.shape, axis)
    return jnp.where(place == (extent - 1 if offset > 0 else 0), 0.0, rolled)


def halo_copies(src, halo, send, recv, me):
    up = pltpu.make_async_remote_copy(
        src_ref=src,
        dst_ref=halo.at[1],
        send_sem=send.at[0],
        recv_sem=recv.at[1],
        device_id={"tile": jnp.maximum(me - 1, 0)},
        device_id_type=MESH,
    )
    down = pltpu.make_async_remote_copy(
        src_ref=src,
        dst_ref=halo.at[0],
        send_sem=send.at[1],
        recv_sem=recv.at[0],
        device_id={"tile": jnp.minimum(me + 1, 15)},
        device_id_type=MESH,
    )
    return up, down


def middle_kernel(
    act_ref,
    clean_ref,
    noise_ref,
    weight_ref,
    kernel_ref,
    flows_ref,
    grad_ref,
    gathered_ref,
    halo_a,
    halo_g,
    gather_send,
    gather_recv,
    a_send,
    a_recv,
    g_send,
    g_recv,
):
    me = lax.axis_index("tile")
    last = 15
    columns = act_ref.shape[0]
    f32 = jnp.float32
    entry_barrier(me, 16)
    a_up, a_down = halo_copies(act_ref, halo_a, a_send, a_recv, me)
    g_up, g_down = halo_copies(grad_ref, halo_g, g_send, g_recv, me)

    @pl.when(me > 0)
    def _():
        a_up.start()

    @pl.when(me < last)
    def _():
        a_down.start()

    gathered_ref[me] = act_ref[...].T
    gather = Gather(gathered_ref, gather_send, gather_recv)
    gather.start()

    @pl.when(me == 0)
    def _():
        halo_a[0] = jnp.zeros_like(halo_a[0])
        halo_g[0] = jnp.zeros_like(halo_g[0])

    @pl.when(me == last)
    def _():
        halo_a[1] = jnp.zeros_like(halo_a[1])
        halo_g[1] = jnp.zeros_like(halo_g[1])

    own = act_ref[...]
    sums = [jnp.dot(own, kernel_ref[3 + d], preferred_element_type=f32) for d in range(3)]

    @pl.when(me > 0)
    def _():
        a_down.wait_recv()

    @pl.when(me < last)
    def _():
        a_up.wait_recv()

    above, below = halo_a[0], halo_a[1]
    sums = [
        sums[d]
        + jnp.dot(above, kernel_ref[d], preferred_element_type=f32)
        + jnp.dot(below, kernel_ref[6 + d], preferred_element_type=f32)
        for d in range(3)
    ]
    predicted = sums[1] + moved(sums[0], -1, 0) + moved(sums[2], 1, 0)
    grad = (
        weight_ref[...]
        * (predicted - clean_ref[...].astype(f32) + noise_ref[...].astype(f32))
        / columns
    ).astype(jnp.bfloat16)
    grad_ref[...] = grad

    @pl.when(me > 0)
    def _():
        g_up.start()

    @pl.when(me < last)
    def _():
        g_down.start()

    def back(values, tap):
        return lax.dot_general(
            values, kernel_ref[tap], (((1,), (1,)), ((), ())), preferred_element_type=f32
        )

    gather.pass_z(1)
    sums = [back(grad, 3 + d) for d in range(3)]
    gather.pass_x(0)
    gather.pass_z(2)

    @pl.when(me > 0)
    def _():
        g_down.wait_recv()

    @pl.when(me < last)
    def _():
        g_up.wait_recv()

    above, below = halo_g[0], halo_g[1]
    sums = [sums[d] + back(below, d) + back(above, 6 + d) for d in range(3)]
    flows_ref[...] = sums[1] + moved(sums[0], 1, 0) + moved(sums[2], -1, 0)
    gather.pass_x(1)
    gather.pass_z(3)
    gather.pass_x(2)
    gather.pass_x(3)
    for step in range(4):
        gather.take(step)
    gather.drain()

    @pl.when(me > 0)
    def _():
        a_up.wait_send()
        g_up.wait_send()

    @pl.when(me < last)
    def _():
        a_down.wait_send()
        g_down.wait_send()


def middle(activated, clean, noise, pixel_weight, kernel):
    pixels, channels = activated.shape
    dma = pltpu.SemaphoreType.DMA
    return pl.pallas_call(
        middle_kernel,
        out_shape=(
            jax.ShapeDtypeStruct((pixels, channels), jnp.float32),
            jax.ShapeDtypeStruct((pixels, channels), jnp.bfloat16),
            jax.ShapeDtypeStruct((16, channels, pixels), jnp.bfloat16),
        ),
        in_specs=[pl.BlockSpec(memory_space=VM)] * 5,
        out_specs=(pl.BlockSpec(memory_space=VM),) * 3,
        scratch_shapes=[
            VM((2, pixels, channels), jnp.bfloat16),
            VM((2, pixels, channels), jnp.bfloat16),
            dma((17,)),
            dma((16,)),
            dma((2,)),
            dma((2,)),
            dma((2,)),
            dma((2,)),
        ],
        compiler_params=pltpu.CompilerParams(
            collective_id=1, has_side_effects=True, vmem_limit_bytes=14 * 2**20
        ),
        name="middle",
    )(activated, clean, noise, pixel_weight, kernel)


def outer_kernel(
    grad_ref,
    gathered_ref,
    parts_ref,
    result_ref,
    total_ref,
    grads,
    shifted,
    sums,
    landed,
    gather_send,
    gather_recv,
    half_send,
    half_recv,
    sum_send,
    sum_recv,
):
    me = lax.axis_index("tile")
    channels, pixels = gathered_ref.shape[1:]
    part = channels // 2
    f32 = jnp.float32
    entry_barrier(me, 16)
    grads[me] = grad_ref[...]
    gather = Gather(grads, gather_send, gather_recv)
    gather.start()
    core, z = gather.core, gather.z
    mine = pl.ds(pl.multiple_of(core * part, part), part)
    rows = parts_ref.shape[0] // 2
    my_rows = pl.ds(pl.multiple_of(core * rows, 8), rows)
    other_rows = pl.ds(pl.multiple_of((1 - core) * rows, 8), rows)
    z_near = (z + 1 - 2 * lax.rem(z, 2)) * 4 + lax.rem(me, 4)
    z_far = lax.rem(z + 2, 4) * 4 + lax.rem(me, 4)

    def sum_copy(src, dst, stage, to):
        return pltpu.make_async_remote_copy(
            src_ref=src,
            dst_ref=dst,
            send_sem=sum_send.at[stage],
            recv_sem=sum_recv.at[stage],
            device_id={"tile": to},
            device_id_type=MESH,
        )

    hops = [
        sum_copy(parts_ref.at[other_rows], landed.at[0], 0, gather.sibling),
        sum_copy(sums.at[0], landed.at[1], 1, gather.x_peer),
        sum_copy(sums.at[1], landed.at[2], 2, z_near),
        sum_copy(sums.at[2], landed.at[3], 3, z_far),
        sum_copy(total_ref.at[my_rows], total_ref.at[my_rows], 4, gather.sibling),
    ]
    hops[0].start()

    def add_hop(stage):
        hops[stage].wait_recv()
        held = parts_ref[my_rows, :] if stage == 0 else sums[stage - 1]
        if stage < 3:
            sums[stage] = held + landed[stage]
        else:
            total_ref[my_rows, :] = held + landed[stage]
        hops[stage + 1].start()

    zeros = jnp.zeros((3 * part, pixels), jnp.bfloat16)
    shifted[:, 0:pixels] = zeros
    shifted[:, 17 * pixels : 18 * pixels] = zeros

    def shift_some(low, high):
        def step(chunk, carry):
            plain = gathered_ref[chunk, mine, :]
            wide = plain.astype(f32)
            here = pl.ds(pl.multiple_of((chunk + 1) * pixels, pixels), pixels)
            shifted[0:part, here] = moved(wide, -1, 1).astype(jnp.bfloat16)
            shifted[part : 2 * part, here] = plain
            shifted[2 * part : 3 * part, here] = moved(wide, 1, 1).astype(jnp.bfloat16)
            return carry

        lax.fori_loop(low, high, step, 0)

    def half_copy(row):
        return pltpu.make_async_remote_copy(
            src_ref=result_ref.at[pl.ds(3 * row, 3), mine],
            dst_ref=result_ref.at[pl.ds(3 * row, 3), mine],
            send_sem=half_send.at[row],
            recv_sem=half_recv.at[row],
            device_id={"tile": gather.sibling},
            device_id_type=MESH,
        )

    def multiply(order):
        base = gather.planes[order] * 4
        right = grads[pl.ds(base, 4)].reshape(4 * pixels, channels)

        def step(row, carry):
            start = pl.multiple_of((base + row) * pixels, pixels)
            left = shifted[:, pl.ds(start, 4 * pixels)]
            product = jnp.dot(left, right, preferred_element_type=f32)
            for d in range(3):
                piece = product[d * part : (d + 1) * part]
                if order == 0:
                    result_ref[3 * row + d, mine, :] = piece
                else:
                    result_ref[3 * row + d, mine, :] = result_ref[3 * row + d, mine, :] + piece
            if order == 3:
                half_copy(row).start()
            return carry

        lax.fori_loop(0, 3, step, 0)

    shift_some(0, 4)
    gather.pass_z(1)
    gather.pass_x(0)
    add_hop(0)
    shift_some(4, 10)
    gather.pass_z(2)
    gather.pass_x(1)
    shift_some(10, 16)
    add_hop(1)
    gather.take(0)
    gather.pass_z(3)
    multiply(0)
    gather.pass_x(2)
    add_hop(2)
    gather.take(1)
    multiply(1)
    gather.pass_x(3)
    add_hop(3)
    gather.take(2)
    multiply(2)
    gather.take(3)
    multiply(3)
    hops[4].wait_recv()
    gather.drain()
    for hop in hops:
        hop.wait_send()
    for row in range(3):
        half_copy(row).wait()


def outer(grad, gathered, parts):
    pixels, channels = grad.shape
    rows = parts.shape[0] // 2
    dma = pltpu.SemaphoreType.DMA
    return pl.pallas_call(
        outer_kernel,
        out_shape=(
            jax.ShapeDtypeStruct((9, channels, channels), jnp.float32),
            jax.ShapeDtypeStruct(parts.shape, jnp.float32),
        ),
        in_specs=[pl.BlockSpec(memory_space=VM)] * 3,
        out_specs=(pl.BlockSpec(memory_space=VM),) * 2,
        scratch_shapes=[
            VM((16, pixels, channels), jnp.bfloat16),
            VM((3 * channels // 2, 18 * pixels), jnp.bfloat16),
            VM((3, rows, 128), jnp.float32),
            VM((4, rows, 128), jnp.float32),
            dma((17,)),
            dma((16,)),
            dma((3,)),
            dma((3,)),
            dma((5,)),
            dma((5,)),
        ],
        compiler_params=pltpu.CompilerParams(
            collective_id=2, has_side_effects=True, vmem_limit_bytes=24 * 2**20
        ),
        name="outer",
    )(grad, gathered, parts)


def body16(
    sar_faces,
    dest_owner,
    face_slot,
    valid_pixels,
    cloud_mask,
    time_index,
    clean_latent,
    noise_latent,
    encoder_first,
    encoder_second,
    conv_kernel,
    norm_gain,
):
    owners = lax.axis_size("tile")
    slot_total = owners * MOST
    face_count, length, channels_in = sar_faces.shape
    rows, columns, channels = clean_latent.shape
    tile_faces = rows * columns // length
    owner_list = dest_owner[:, 0]
    onehot = (owner_list[:, None] == jnp.arange(owners, dtype=jnp.int32)[None, :]).astype(jnp.int32)
    before = jnp.cumsum(onehot, axis=0) - onehot
    within = jnp.sum(before * onehot, axis=1)
    buffer_at = owner_list * MOST + within
    placed = (jnp.arange(slot_total, dtype=jnp.int32)[:, None] == buffer_at[None, :]).astype(
        jnp.int32
    )
    placer = placed.astype(jnp.bfloat16)
    labels = jnp.stack(
        [
            jnp.sum(placed * face_slot[None, :], axis=1),
            jnp.sum(placed * valid_pixels[None, :], axis=1),
        ],
        axis=-1,
    )
    packed = jnp.einsum(
        "sf,fjc->sjc", placer, sar_faces, preferred_element_type=jnp.float32
    ).astype(jnp.bfloat16)
    label_rows = jnp.pad(
        labels.astype(jnp.bfloat16)[:, None, :],
        ((0, 0), (0, length - 1), (0, channels_in - 2)),
    )
    arrived = exchange(
        jnp.concatenate([packed, label_rows], axis=1).reshape(
            owners, MOST * 2 * length, channels_in
        )
    ).reshape(slot_total, 2 * length, channels_in)
    raw_slots = arrived[:, :length]
    recv_labels = arrived[:, length, :2].astype(jnp.int32)
    received, saved = encoder_forward(raw_slots, encoder_first, encoder_second)
    recv_slot = recv_labels[:, 0]
    recv_count = recv_labels[:, 1]
    validity = (jnp.arange(length, dtype=jnp.int32)[None, :] < recv_count[:, None]).astype(
        jnp.float32
    )
    selector = recv_slot[:, None] == jnp.arange(tile_faces, dtype=jnp.int32)[None, :]
    masked = received * validity[..., None].astype(jnp.bfloat16)
    summed = jnp.einsum(
        "sp,sjc->pjc", selector.astype(jnp.bfloat16), masked, preferred_element_type=jnp.float32
    )
    covered = jnp.einsum(
        "sp,sj->pj", selector.astype(jnp.float32), validity, precision=highest
    ).reshape(-1, 1)
    condition = summed.reshape(-1, channels) / (1.0 + covered)
    time_value = (time_index[0].astype(jnp.float32) + 0.5) / NSTEPS
    noise_flat = noise_latent.astype(jnp.float32).reshape(-1, channels)
    clean_flat = clean_latent.astype(jnp.float32).reshape(-1, channels)
    hsum = (1.0 - time_value) * noise_flat + time_value * clean_flat + condition
    inverse = lax.rsqrt(jnp.mean(hsum * hsum, axis=-1, keepdims=True) + epsilon)
    normed = hsum * inverse
    lifted = normed * norm_gain
    activated = jax.nn.silu(lifted).astype(jnp.bfloat16)
    pixel_weight = (1 + cloud_mask).astype(jnp.float32).reshape(-1, 1)
    flows, grad_pred, gathered = middle(
        activated,
        clean_latent.reshape(-1, channels),
        noise_latent.reshape(-1, channels),
        pixel_weight,
        conv_kernel,
    )
    gain_part, grad_hsum = norm_backward(flows, lifted, normed, inverse, norm_gain)
    scaled = (grad_hsum / (1.0 + covered)).reshape(tile_faces, length, channels)
    slot_grads = (jnp.take(scaled, recv_slot, axis=0) * validity[..., None]).astype(jnp.bfloat16)
    first_part, second_part = encoder_backward(saved, slot_grads, encoder_first, encoder_second)
    parts = (second_part, first_part, gain_part)
    flat = jnp.concatenate([part.reshape(-1, 128) for part in parts], axis=0)
    flat = jnp.pad(flat, ((0, -flat.shape[0] % 16), (0, 0)))
    grad_kernel, total = outer(grad_pred, gathered, flat)
    sums = []
    at = 0
    for part in parts:
        count = part.size // 128
        sums.append(total[at : at + count].reshape(part.shape))
        at += count
    return (grad_kernel, sums[2], sums[1], sums[0])


def body(
    sar_faces,
    dest_owner,
    face_slot,
    valid_pixels,
    cloud_mask,
    time_index,
    clean_latent,
    noise_latent,
    encoder_first,
    encoder_second,
    conv_kernel,
    norm_gain,
):
    owners = lax.axis_size("tile")
    slot_total = owners * MOST
    face_count, length, channels_in = sar_faces.shape
    rows, columns, channels = clean_latent.shape
    tile_faces = rows * columns // length
    owner_list = dest_owner[:, 0]
    onehot = (owner_list[:, None] == jnp.arange(owners, dtype=jnp.int32)[None, :]).astype(jnp.int32)
    before = jnp.cumsum(onehot, axis=0) - onehot
    within = jnp.sum(before * onehot, axis=1)
    buffer_at = owner_list * MOST + within
    placed = (jnp.arange(slot_total, dtype=jnp.int32)[:, None] == buffer_at[None, :]).astype(
        jnp.int32
    )
    placer = placed.astype(jnp.bfloat16)
    labels = jnp.stack(
        [
            jnp.sum(placed * face_slot[None, :], axis=1),
            jnp.sum(placed * valid_pixels[None, :], axis=1),
        ],
        axis=-1,
    )
    labels = labels.reshape(owners, MOST, 2)
    packed = jnp.einsum(
        "sf,fjc->sjc", placer, sar_faces, preferred_element_type=jnp.float32
    ).astype(jnp.bfloat16)
    arrived, recv_labels = (
        lax.all_to_all(
            packed.reshape(owners, MOST, length, channels_in),
            "tile",
            split_axis=0,
            concat_axis=0,
            tiled=True,
        ),
        lax.all_to_all(labels, "tile", split_axis=0, concat_axis=0, tiled=True),
    )
    raw_slots = arrived.reshape(slot_total, length, channels_in)
    received, saved = encoder_forward(raw_slots, encoder_first, encoder_second)
    recv_labels = recv_labels.reshape(slot_total, 2)
    recv_slot = recv_labels[:, 0]
    recv_count = recv_labels[:, 1]
    validity = (jnp.arange(length, dtype=jnp.int32)[None, :] < recv_count[:, None]).astype(
        jnp.float32
    )
    selector = recv_slot[:, None] == jnp.arange(tile_faces, dtype=jnp.int32)[None, :]
    masked = received * validity[..., None].astype(jnp.bfloat16)
    summed = jnp.einsum(
        "sp,sjc->pjc", selector.astype(jnp.bfloat16), masked, preferred_element_type=jnp.float32
    )
    covered = jnp.einsum(
        "sp,sj->pj", selector.astype(jnp.float32), validity, precision=highest
    ).reshape(-1, 1)
    condition = summed.reshape(-1, channels) / (1.0 + covered)
    time_value = (time_index[0].astype(jnp.float32) + 0.5) / NSTEPS
    noise_flat = noise_latent.astype(jnp.float32).reshape(-1, channels)
    clean_flat = clean_latent.astype(jnp.float32).reshape(-1, channels)
    hsum = (1.0 - time_value) * noise_flat + time_value * clean_flat + condition
    inverse = lax.rsqrt(jnp.mean(hsum * hsum, axis=-1, keepdims=True) + epsilon)
    normed = hsum * inverse
    lifted = normed * norm_gain
    activated = jax.nn.silu(lifted).astype(jnp.bfloat16).reshape(rows, columns, channels)
    extended = with_halo(activated, (("tile", 0),), 1)
    padded = jnp.pad(extended, ((0, 0), (1, 1), (0, 0)))
    predicted = convolve_forward(padded, conv_kernel, rows, columns)
    pixel_weight = (1 + cloud_mask).astype(jnp.float32).reshape(-1, 1)
    grad_pred = (pixel_weight * (predicted - clean_flat + noise_flat) / (rows * columns)).astype(
        jnp.bfloat16
    )
    grad_rows = with_halo(grad_pred.reshape(rows, columns, channels), (("tile", 0),), 1)
    padded_grad = jnp.pad(grad_rows, ((0, 0), (1, 1), (0, 0)))
    flows, kernel_part = convolve_backward(padded, padded_grad, conv_kernel, rows, columns)
    gain_part, grad_hsum = norm_backward(flows, lifted, normed, inverse, norm_gain)
    scaled = (grad_hsum / (1.0 + covered)).reshape(tile_faces, length, channels)
    slot_grads = (jnp.take(scaled, recv_slot, axis=0) * validity[..., None]).astype(jnp.bfloat16)
    first_part, second_part = encoder_backward(saved, slot_grads, encoder_first, encoder_second)
    reduced = lax.psum((kernel_part, gain_part, first_part, second_part), "tile")
    return (reduced[0], reduced[1], reduced[2], reduced[3])


def solution(mesh):
    placed = (
        P(("groups", "tile"), None, None),
        P(("groups", "tile"), None),
        P(("groups", "tile")),
        P(("groups", "tile")),
        P(("groups", "tile"), None),
        P(("groups", "tile")),
        P(("groups", "tile"), None, None),
        P(("groups", "tile"), None, None),
        P(),
        P(),
        P(),
        P(),
    )
    return jax.shard_map(
        body16 if mesh.shape["tile"] == 16 else body,
        mesh=mesh,
        in_specs=placed,
        out_specs=(
            P("groups", None, None),
            P("groups"),
            P("groups", None, None, None),
            P("groups", None, None, None),
        ),
        check_vma=False,
    )
```

```python
import jax
import jax.numpy as jnp
from jax import lax
from jax.experimental import pallas as pl
from jax.experimental.pallas import tpu as pltpu
from jax.sharding import PartitionSpec as P

MOST = 2
NSTEPS = 1000


highest = lax.Precision.HIGHEST
epsilon = 1e-06


def with_halo(block, sides, width):
    for axis, dim in sides:
        count = lax.axis_size(axis)
        forward = [(i, i + 1) for i in range(count - 1)]
        backward = [(target, source) for source, target in forward]
        low = lax.ppermute(
            lax.slice_in_dim(block, block.shape[dim] - width, None, axis=dim), axis, forward
        )
        high = lax.ppermute(lax.slice_in_dim(block, 0, width, axis=dim), axis, backward)
        block = jnp.concatenate([low, block, high], axis=dim)
    return block


def shift_line(values, offset):
    if offset == 0:
        return values
    zeros = jnp.zeros_like(values[:, : abs(offset)])
    if offset > 0:
        return jnp.concatenate([values[:, offset:], zeros], axis=1)
    return jnp.concatenate([zeros, values[:, :offset]], axis=1)


def taps_forward(inputs, weight, spread):
    summed = jnp.zeros(inputs.shape[:3] + (weight.shape[-1],), jnp.float32)
    for shift_tap in range(3):
        shifted = shift_line(inputs, (shift_tap - 1) * spread)
        summed = summed + jnp.einsum(
            "flgi,gio->flgo", shifted, weight[shift_tap], preferred_element_type=jnp.float32
        )
    return summed


def taps_weight_grad(inputs, cotangent, spread, exact):
    pieces = []
    for shift_tap in range(3):
        shifted = shift_line(inputs, (shift_tap - 1) * spread)
        if exact:
            pieces.append(
                jnp.einsum(
                    "flgi,flgo->gio", shifted.astype(jnp.float32), cotangent, precision=highest
                )
            )
        else:
            pieces.append(
                jnp.einsum("flgi,flgo->gio", shifted, cotangent, preferred_element_type=jnp.float32)
            )
    return jnp.stack(pieces)


def taps_input_grad(cotangent, weight, spread):
    summed = jnp.zeros(cotangent.shape[:3] + (weight.shape[2],), jnp.float32)
    for shift_tap in range(3):
        moved = jnp.einsum(
            "flgo,gio->flgi", cotangent, weight[shift_tap], preferred_element_type=jnp.float32
        )
        summed = summed + shift_line(moved, -(shift_tap - 1) * spread)
    return summed


def encoder_forward(sar_faces, first_w, second_w):
    face_count, length, channels_in = sar_faces.shape
    groups = first_w.shape[1]
    inputs = sar_faces.reshape(face_count, length, groups, -1)
    first_out = taps_forward(inputs, first_w, 1)
    hidden = jax.nn.silu(first_out).astype(jnp.bfloat16)
    second = taps_forward(hidden, second_w, 2)
    encoded = (
        (hidden.astype(jnp.float32) + second).reshape(face_count, length, -1).astype(jnp.bfloat16)
    )
    return (encoded, (inputs, first_out, hidden))


def encoder_backward(saved, grad_face, first_w, second_w):
    inputs, first_out, hidden = saved
    groups = first_w.shape[1]
    face_count, length, channels = grad_face.shape
    cotangent = grad_face.reshape(face_count, length, groups, -1)
    second_part = taps_weight_grad(hidden, cotangent, 2, False)
    grad_hidden = cotangent.astype(jnp.float32) + taps_input_grad(cotangent, second_w, 2)
    logistic = jax.nn.sigmoid(first_out)
    grad_first_out = grad_hidden * logistic * (1.0 + first_out * (1.0 - logistic))
    first_part = taps_weight_grad(inputs, grad_first_out, 1, True)
    return (first_part, second_part)


def convolve_forward(padded, kernel, rows, columns):
    channels = kernel.shape[-1]
    summed = jnp.zeros((rows * columns, channels), jnp.float32)
    for row_tap in range(3):
        for col_tap in range(3):
            window = padded[row_tap : row_tap + rows, col_tap : col_tap + columns].reshape(
                -1, channels
            )
            summed = summed + jnp.dot(
                window, kernel[3 * row_tap + col_tap], preferred_element_type=jnp.float32
            )
    return summed


def convolve_backward(padded_act, padded_grad, kernel, rows, columns):
    channels = kernel.shape[-1]
    incoming = padded_grad[1 : rows + 1, 1 : columns + 1].reshape(-1, channels)
    flows = jnp.zeros((rows * columns, channels), jnp.float32)
    kernels = []
    for row_tap in range(3):
        for col_tap in range(3):
            window = padded_act[row_tap : row_tap + rows, col_tap : col_tap + columns].reshape(
                -1, channels
            )
            kernels.append(
                lax.dot_general(
                    window, incoming, (((0,), (0,)), ((), ())), preferred_element_type=jnp.float32
                )
            )
            moved = padded_grad[
                2 - row_tap : 2 - row_tap + rows, 2 - col_tap : 2 - col_tap + columns
            ].reshape(-1, channels)
            flows = flows + lax.dot_general(
                moved,
                kernel[3 * row_tap + col_tap],
                (((1,), (1,)), ((), ())),
                preferred_element_type=jnp.float32,
            )
    return (flows, jnp.stack(kernels))


def norm_backward(flows, lifted, normed, inverse, gain):
    logistic = jax.nn.sigmoid(lifted)
    grad_lift = flows * logistic * (1.0 + lifted * (1.0 - logistic))
    gain_part = jnp.sum(grad_lift * normed, axis=0)
    grad_norm = grad_lift * gain
    grad_hsum = inverse * (
        grad_norm - normed * jnp.mean(grad_norm * normed, axis=-1, keepdims=True)
    )
    return (gain_part, grad_hsum)


MESH = pl.DeviceIdType.MESH
VM = pltpu.VMEM


def entry_barrier(me, count):
    barrier = pltpu.get_barrier_semaphore()
    for k in range(1, count):
        pl.semaphore_signal(
            barrier, inc=1, device_id={"tile": lax.rem(me + k, count)}, device_id_type=MESH
        )
    pl.semaphore_wait(barrier, count - 1)


def exchange_kernel(count, x_ref, o_ref, send, recv, local):
    me = lax.axis_index("tile")
    entry_barrier(me, count)
    own = pltpu.make_async_copy(x_ref.at[me], o_ref.at[me], local)
    own.start()
    copies = []
    for k in range(1, count):
        to = lax.rem(me + k, count)
        copy = pltpu.make_async_remote_copy(
            src_ref=x_ref.at[to],
            dst_ref=o_ref.at[me],
            send_sem=send.at[k - 1],
            recv_sem=recv.at[k - 1],
            device_id={"tile": to},
            device_id_type=MESH,
        )
        copy.start()
        copies.append(copy)
    own.wait()
    for copy in copies:
        copy.wait()


def exchange(packed):
    count = packed.shape[0]
    return pl.pallas_call(
        lambda *refs: exchange_kernel(count, *refs),
        out_shape=jax.ShapeDtypeStruct(packed.shape, packed.dtype),
        in_specs=[pl.BlockSpec(memory_space=VM)],
        out_specs=pl.BlockSpec(memory_space=VM),
        scratch_shapes=[
            pltpu.SemaphoreType.DMA((count - 1,)),
            pltpu.SemaphoreType.DMA((count - 1,)),
            pltpu.SemaphoreType.DMA,
        ],
        compiler_params=pltpu.CompilerParams(collective_id=0, has_side_effects=True),
        name="exchange",
    )(packed)


class Gather:
    def __init__(self, buf, send, recv):
        self.buf, self.send_sem, self.recv_sem = buf, send, recv
        self.me = lax.axis_index("tile")
        self.core = lax.rem(self.me, 2)
        self.x = lax.rem(self.me // 2, 2)
        self.z = z = self.me // 4
        self.x_peer = z * 4 + (1 - self.x) * 2 + self.core
        self.sibling = z * 4 + self.x * 2 + (1 - self.core)
        self.planes = [
            z,
            jnp.where(z == 0, 1, z - 1),
            jnp.where(z == 0, 2, jnp.where(z == 3, 1, z + 1)),
            jnp.where(z < 2, 3, 0),
        ]

    def copy(self, chunk, to, index):
        return pltpu.make_async_remote_copy(
            src_ref=self.buf.at[chunk],
            dst_ref=self.buf.at[chunk],
            send_sem=self.send_sem.at[index],
            recv_sem=self.recv_sem.at[chunk],
            device_id={"tile": to},
            device_id_type=MESH,
        )

    def at(self, step, x, core):
        return self.planes[step] * 4 + x * 2 + core

    def along(self, step):
        place = lax.rem(self.me, 4)
        onward = jnp.where(self.planes[step] < self.z, self.z + 1, self.z - 1)
        valid = (onward >= 0) & (onward <= 3)
        return jnp.clip(onward, 0, 3) * 4 + place, valid

    def start(self):
        place = lax.rem(self.me, 4)

        @pl.when(self.z < 3)
        def _():
            self.copy(self.me, jnp.minimum(self.z + 1, 3) * 4 + place, 0).start()

        @pl.when(self.z > 0)
        def _():
            self.copy(self.me, jnp.maximum(self.z - 1, 0) * 4 + place, 1).start()

        self.copy(self.me, self.x_peer, 2).start()
        self.copy(self.me, self.sibling, 3).start()

    def pass_z(self, step):
        chunk = self.at(step, self.x, self.core)
        self.copy(chunk, self.x_peer, 0).wait_recv()
        to, valid = self.along(step)

        @pl.when(valid)
        def _():
            self.copy(chunk, to, 3 + step).start()

        self.copy(chunk, self.x_peer, 6 + step).start()
        self.copy(chunk, self.sibling, 9 + step).start()

    def pass_x(self, step):
        chunk = self.at(step, 1 - self.x, self.core)
        self.copy(chunk, self.sibling, 0).wait_recv()
        self.copy(chunk, self.sibling, 13 + step).start()

    def take(self, step):
        for x in (self.x, 1 - self.x):
            chunk = self.at(step, x, 1 - self.core)
            self.copy(chunk, self.sibling, 0).wait_recv()

    def drain(self):
        @pl.when(self.z < 3)
        def _():
            self.copy(self.me, self.sibling, 0).wait_send()

        @pl.when(self.z > 0)
        def _():
            self.copy(self.me, self.sibling, 1).wait_send()

        for step in range(1, 4):
            _, valid = self.along(step)

            @pl.when(valid)
            def _():
                self.copy(self.me, self.sibling, 3 + step).wait_send()

        for index in (2, 3, 7, 8, 9, 10, 11, 12, 13, 14, 15, 16):
            self.copy(self.me, self.sibling, index).wait_send()


class Spread:
    def __init__(self, buf, send, recv):
        self.buf, self.send_sem, self.recv_sem = buf, send, recv
        self.me = lax.axis_index("tile")
        self.core = lax.rem(self.me, 2)
        self.x = lax.rem(self.me // 2, 2)
        self.z = self.me // 4
        self.x_peer = self.z * 4 + (1 - self.x) * 2 + self.core
        self.sibling = self.z * 4 + self.x * 2 + (1 - self.core)

    def copy(self, chunk, to, index):
        return pltpu.make_async_remote_copy(
            src_ref=self.buf.at[chunk],
            dst_ref=self.buf.at[chunk],
            send_sem=self.send_sem.at[index],
            recv_sem=self.recv_sem.at[chunk],
            device_id={"tile": to},
            device_id_type=MESH,
        )

    def at(self, back, x, core):
        return lax.rem(self.z + 4 - back, 4) * 4 + x * 2 + core

    def start(self):
        self.copy(self.me, self.x_peer, 3).start()
        self.copy(self.me, self.sibling, 4).start()
        for k in (1, 3, 2):
            to = lax.rem(self.z + k, 4) * 4 + self.x * 2 + self.core
            self.copy(self.me, to, k - 1).start()

    def pass_z(self, back):
        chunk = self.at(back, self.x, self.core)
        self.copy(chunk, self.x_peer, 0).wait_recv()
        self.copy(chunk, self.x_peer, 5 + 2 * (back - 1)).start()
        self.copy(chunk, self.sibling, 6 + 2 * (back - 1)).start()

    def pass_x(self, back):
        chunk = self.at(back, 1 - self.x, self.core)
        self.copy(chunk, self.sibling, 0).wait_recv()
        self.copy(chunk, self.sibling, 11 + back).start()

    def take(self, back):
        for x in (self.x, 1 - self.x):
            chunk = self.at(back, x, 1 - self.core)
            self.copy(chunk, self.sibling, 0).wait_recv()

    def drain(self):
        for index in range(15):
            self.copy(self.me, self.sibling, index).wait_send()


def moved(values, offset, axis):
    extent = values.shape[axis]
    rolled = pltpu.roll(values, (-offset) % extent, axis)
    place = lax.broadcasted_iota(jnp.int32, values.shape, axis)
    return jnp.where(place == (extent - 1 if offset > 0 else 0), 0.0, rolled)


def halo_copies(src, halo, send, recv, me):
    up = pltpu.make_async_remote_copy(
        src_ref=src,
        dst_ref=halo.at[1],
        send_sem=send.at[0],
        recv_sem=recv.at[1],
        device_id={"tile": jnp.maximum(me - 1, 0)},
        device_id_type=MESH,
    )
    down = pltpu.make_async_remote_copy(
        src_ref=src,
        dst_ref=halo.at[0],
        send_sem=send.at[1],
        recv_sem=recv.at[0],
        device_id={"tile": jnp.minimum(me + 1, 15)},
        device_id_type=MESH,
    )
    return up, down


def middle_kernel(
    act_ref,
    clean_ref,
    noise_ref,
    weight_ref,
    kernel_ref,
    flows_ref,
    grad_ref,
    gathered_ref,
    halo_a,
    halo_g,
    gather_send,
    gather_recv,
    a_send,
    a_recv,
    g_send,
    g_recv,
):
    me = lax.axis_index("tile")
    last = 15
    columns = act_ref.shape[0]
    f32 = jnp.float32
    entry_barrier(me, 16)
    a_up, a_down = halo_copies(act_ref, halo_a, a_send, a_recv, me)
    g_up, g_down = halo_copies(grad_ref, halo_g, g_send, g_recv, me)

    @pl.when(me > 0)
    def _():
        a_up.start()

    @pl.when(me < last)
    def _():
        a_down.start()

    gathered_ref[me] = act_ref[...].T
    gather = Spread(gathered_ref, gather_send, gather_recv)
    gather.start()

    @pl.when(me == 0)
    def _():
        halo_a[0] = jnp.zeros_like(halo_a[0])
        halo_g[0] = jnp.zeros_like(halo_g[0])

    @pl.when(me == last)
    def _():
        halo_a[1] = jnp.zeros_like(halo_a[1])
        halo_g[1] = jnp.zeros_like(halo_g[1])

    own = act_ref[...]
    sums = [jnp.dot(own, kernel_ref[3 + d], preferred_element_type=f32) for d in range(3)]

    @pl.when(me > 0)
    def _():
        a_down.wait_recv()

    @pl.when(me < last)
    def _():
        a_up.wait_recv()

    above, below = halo_a[0], halo_a[1]
    sums = [
        sums[d]
        + jnp.dot(above, kernel_ref[d], preferred_element_type=f32)
        + jnp.dot(below, kernel_ref[6 + d], preferred_element_type=f32)
        for d in range(3)
    ]
    predicted = sums[1] + moved(sums[0], -1, 0) + moved(sums[2], 1, 0)
    grad = (
        weight_ref[...]
        * (predicted - clean_ref[...].astype(f32) + noise_ref[...].astype(f32))
        / columns
    ).astype(jnp.bfloat16)
    grad_ref[...] = grad

    @pl.when(me > 0)
    def _():
        g_up.start()

    @pl.when(me < last)
    def _():
        g_down.start()

    def back(values, tap):
        return lax.dot_general(
            values, kernel_ref[tap], (((1,), (1,)), ((), ())), preferred_element_type=f32
        )

    sums = [back(grad, 3 + d) for d in range(3)]
    for k in (1, 3, 2):
        gather.pass_z(k)

    @pl.when(me > 0)
    def _():
        g_down.wait_recv()

    @pl.when(me < last)
    def _():
        g_up.wait_recv()

    above, below = halo_g[0], halo_g[1]
    sums = [sums[d] + back(below, d) + back(above, 6 + d) for d in range(3)]
    flows_ref[...] = sums[1] + moved(sums[0], 1, 0) + moved(sums[2], -1, 0)
    for k in (0, 1, 3, 2):
        gather.pass_x(k)
    for k in (0, 1, 3, 2):
        gather.take(k)
    gather.drain()

    @pl.when(me > 0)
    def _():
        a_up.wait_send()
        g_up.wait_send()

    @pl.when(me < last)
    def _():
        a_down.wait_send()
        g_down.wait_send()


def middle(activated, clean, noise, pixel_weight, kernel):
    pixels, channels = activated.shape
    dma = pltpu.SemaphoreType.DMA
    return pl.pallas_call(
        middle_kernel,
        out_shape=(
            jax.ShapeDtypeStruct((pixels, channels), jnp.float32),
            jax.ShapeDtypeStruct((pixels, channels), jnp.bfloat16),
            jax.ShapeDtypeStruct((16, channels, pixels), jnp.bfloat16),
        ),
        in_specs=[pl.BlockSpec(memory_space=VM)] * 5,
        out_specs=(pl.BlockSpec(memory_space=VM),) * 3,
        scratch_shapes=[
            VM((2, pixels, channels), jnp.bfloat16),
            VM((2, pixels, channels), jnp.bfloat16),
            dma((15,)),
            dma((16,)),
            dma((2,)),
            dma((2,)),
            dma((2,)),
            dma((2,)),
        ],
        compiler_params=pltpu.CompilerParams(
            collective_id=1, has_side_effects=True, vmem_limit_bytes=14 * 2**20
        ),
        name="middle",
    )(activated, clean, noise, pixel_weight, kernel)


def outer_kernel(
    grad_ref,
    gathered_ref,
    parts_ref,
    result_ref,
    total_ref,
    grads,
    shifted,
    sums,
    landed,
    gather_send,
    gather_recv,
    half_send,
    half_recv,
    sum_send,
    sum_recv,
):
    me = lax.axis_index("tile")
    channels, pixels = gathered_ref.shape[1:]
    part = channels // 2
    f32 = jnp.float32
    entry_barrier(me, 16)
    grads[me] = grad_ref[...]
    gather = Gather(grads, gather_send, gather_recv)
    gather.start()
    core, z = gather.core, gather.z
    mine = pl.ds(pl.multiple_of(core * part, part), part)
    rows = parts_ref.shape[0] // 2
    my_rows = pl.ds(pl.multiple_of(core * rows, 8), rows)
    other_rows = pl.ds(pl.multiple_of((1 - core) * rows, 8), rows)
    z_near = (z + 1 - 2 * lax.rem(z, 2)) * 4 + lax.rem(me, 4)
    z_far = lax.rem(z + 2, 4) * 4 + lax.rem(me, 4)

    def sum_copy(src, dst, stage, to):
        return pltpu.make_async_remote_copy(
            src_ref=src,
            dst_ref=dst,
            send_sem=sum_send.at[stage],
            recv_sem=sum_recv.at[stage],
            device_id={"tile": to},
            device_id_type=MESH,
        )

    hops = [
        sum_copy(parts_ref.at[other_rows], landed.at[0], 0, gather.sibling),
        sum_copy(sums.at[0], landed.at[1], 1, gather.x_peer),
        sum_copy(sums.at[1], landed.at[2], 2, z_near),
        sum_copy(sums.at[2], landed.at[3], 3, z_far),
        sum_copy(total_ref.at[my_rows], total_ref.at[my_rows], 4, gather.sibling),
    ]
    hops[0].start()

    def add_hop(stage):
        hops[stage].wait_recv()
        held = parts_ref[my_rows, :] if stage == 0 else sums[stage - 1]
        if stage < 3:
            sums[stage] = held + landed[stage]
        else:
            total_ref[my_rows, :] = held + landed[stage]
        hops[stage + 1].start()

    zeros = jnp.zeros((3 * part, pixels), jnp.bfloat16)
    shifted[:, 0:pixels] = zeros
    shifted[:, 17 * pixels : 18 * pixels] = zeros

    def shift_some(low, high):
        def step(chunk, carry):
            plain = gathered_ref[chunk, mine, :]
            wide = plain.astype(f32)
            here = pl.ds(pl.multiple_of((chunk + 1) * pixels, pixels), pixels)
            shifted[0:part, here] = moved(wide, -1, 1).astype(jnp.bfloat16)
            shifted[part : 2 * part, here] = plain
            shifted[2 * part : 3 * part, here] = moved(wide, 1, 1).astype(jnp.bfloat16)
            return carry

        lax.fori_loop(low, high, step, 0)

    def half_copy(row):
        return pltpu.make_async_remote_copy(
            src_ref=result_ref.at[pl.ds(3 * row, 3), mine],
            dst_ref=result_ref.at[pl.ds(3 * row, 3), mine],
            send_sem=half_send.at[row],
            recv_sem=half_recv.at[row],
            device_id={"tile": gather.sibling},
            device_id_type=MESH,
        )

    def multiply(order):
        base = gather.planes[order] * 4
        right = grads[pl.ds(base, 4)].reshape(4 * pixels, channels)

        def step(row, carry):
            start = pl.multiple_of((base + row) * pixels, pixels)
            left = shifted[:, pl.ds(start, 4 * pixels)]
            product = jnp.dot(left, right, preferred_element_type=f32)
            for d in range(3):
                piece = product[d * part : (d + 1) * part]
                if order == 0:
                    result_ref[3 * row + d, mine, :] = piece
                else:
                    result_ref[3 * row + d, mine, :] = result_ref[3 * row + d, mine, :] + piece
            if order == 3:
                half_copy(row).start()
            return carry

        lax.fori_loop(0, 3, step, 0)

    shift_some(0, 4)
    gather.pass_z(1)
    gather.pass_x(0)
    add_hop(0)
    shift_some(4, 10)
    gather.pass_z(2)
    gather.pass_x(1)
    shift_some(10, 16)
    add_hop(1)
    gather.take(0)
    gather.pass_z(3)
    multiply(0)
    gather.pass_x(2)
    add_hop(2)
    gather.take(1)
    multiply(1)
    gather.pass_x(3)
    add_hop(3)
    gather.take(2)
    multiply(2)
    gather.take(3)
    multiply(3)
    hops[4].wait_recv()
    gather.drain()
    for hop in hops:
        hop.wait_send()
    for row in range(3):
        half_copy(row).wait()


def outer(grad, gathered, parts):
    pixels, channels = grad.shape
    rows = parts.shape[0] // 2
    dma = pltpu.SemaphoreType.DMA
    return pl.pallas_call(
        outer_kernel,
        out_shape=(
            jax.ShapeDtypeStruct((9, channels, channels), jnp.float32),
            jax.ShapeDtypeStruct(parts.shape, jnp.float32),
        ),
        in_specs=[pl.BlockSpec(memory_space=VM)] * 3,
        out_specs=(pl.BlockSpec(memory_space=VM),) * 2,
        scratch_shapes=[
            VM((16, pixels, channels), jnp.bfloat16),
            VM((3 * channels // 2, 18 * pixels), jnp.bfloat16),
            VM((3, rows, 128), jnp.float32),
            VM((4, rows, 128), jnp.float32),
            dma((17,)),
            dma((16,)),
            dma((3,)),
            dma((3,)),
            dma((5,)),
            dma((5,)),
        ],
        compiler_params=pltpu.CompilerParams(
            collective_id=2, has_side_effects=True, vmem_limit_bytes=24 * 2**20
        ),
        name="outer",
    )(grad, gathered, parts)


def settle_kernel(x_ref, o_ref, sems):
    count = x_ref.shape[0]
    for i in range(count):
        pltpu.make_async_copy(x_ref.at[i], o_ref.at[i], sems.at[i]).start()
    for i in range(count):
        pltpu.make_async_copy(x_ref.at[i], o_ref.at[i], sems.at[i]).wait()


def settle(values):
    return pl.pallas_call(
        settle_kernel,
        out_shape=jax.ShapeDtypeStruct(values.shape, values.dtype),
        in_specs=[pl.BlockSpec(memory_space=VM)],
        out_specs=pl.BlockSpec(memory_space=pl.ANY),
        scratch_shapes=[pltpu.SemaphoreType.DMA((values.shape[0],))],
        name="settle",
    )(values)


def body16(
    sar_faces,
    dest_owner,
    face_slot,
    valid_pixels,
    cloud_mask,
    time_index,
    clean_latent,
    noise_latent,
    encoder_first,
    encoder_second,
    conv_kernel,
    norm_gain,
):
    owners = lax.axis_size("tile")
    slot_total = owners * MOST
    face_count, length, channels_in = sar_faces.shape
    rows, columns, channels = clean_latent.shape
    tile_faces = rows * columns // length
    owner_list = dest_owner[:, 0]
    onehot = (owner_list[:, None] == jnp.arange(owners, dtype=jnp.int32)[None, :]).astype(jnp.int32)
    before = jnp.cumsum(onehot, axis=0) - onehot
    within = jnp.sum(before * onehot, axis=1)
    buffer_at = owner_list * MOST + within
    placed = (jnp.arange(slot_total, dtype=jnp.int32)[:, None] == buffer_at[None, :]).astype(
        jnp.int32
    )
    placer = placed.astype(jnp.bfloat16)
    labels = jnp.stack(
        [
            jnp.sum(placed * face_slot[None, :], axis=1),
            jnp.sum(placed * valid_pixels[None, :], axis=1),
        ],
        axis=-1,
    )
    packed = jnp.einsum(
        "sf,fjc->sjc", placer, sar_faces, preferred_element_type=jnp.float32
    ).astype(jnp.bfloat16)
    label_rows = jnp.pad(
        labels.astype(jnp.bfloat16)[:, None, :],
        ((0, 0), (0, length - 1), (0, channels_in - 2)),
    )
    arrived = exchange(
        jnp.concatenate([packed, label_rows], axis=1).reshape(
            owners, MOST * 2 * length, channels_in
        )
    ).reshape(slot_total, 2 * length, channels_in)
    raw_slots = arrived[:, :length]
    recv_labels = arrived[:, length, :2].astype(jnp.int32)
    received, saved = encoder_forward(raw_slots, encoder_first, encoder_second)
    recv_slot = recv_labels[:, 0]
    recv_count = recv_labels[:, 1]
    validity = (jnp.arange(length, dtype=jnp.int32)[None, :] < recv_count[:, None]).astype(
        jnp.float32
    )
    selector = recv_slot[:, None] == jnp.arange(tile_faces, dtype=jnp.int32)[None, :]
    masked = received * validity[..., None].astype(jnp.bfloat16)
    summed = jnp.einsum(
        "sp,sjc->pjc", selector.astype(jnp.bfloat16), masked, preferred_element_type=jnp.float32
    )
    covered = jnp.einsum(
        "sp,sj->pj", selector.astype(jnp.float32), validity, precision=highest
    ).reshape(-1, 1)
    condition = summed.reshape(-1, channels) / (1.0 + covered)
    time_value = (time_index[0].astype(jnp.float32) + 0.5) / NSTEPS
    noise_flat = noise_latent.astype(jnp.float32).reshape(-1, channels)
    clean_flat = clean_latent.astype(jnp.float32).reshape(-1, channels)
    hsum = (1.0 - time_value) * noise_flat + time_value * clean_flat + condition
    inverse = lax.rsqrt(jnp.mean(hsum * hsum, axis=-1, keepdims=True) + epsilon)
    normed = hsum * inverse
    lifted = normed * norm_gain
    activated = jax.nn.silu(lifted).astype(jnp.bfloat16)
    pixel_weight = (1 + cloud_mask).astype(jnp.float32).reshape(-1, 1)
    flows, grad_pred, gathered = middle(
        activated,
        clean_latent.reshape(-1, channels),
        noise_latent.reshape(-1, channels),
        pixel_weight,
        conv_kernel,
    )
    gain_part, grad_hsum = norm_backward(flows, lifted, normed, inverse, norm_gain)
    scaled = (grad_hsum / (1.0 + covered)).astype(jnp.bfloat16)
    target = recv_slot[:, None] * length + jnp.arange(length, dtype=jnp.int32)[None, :]
    target = jnp.where(validity > 0, target, -1).reshape(-1)
    picker = target[:, None] == jnp.arange(rows * columns, dtype=jnp.int32)[None, :]
    slot_grads = jnp.dot(
        picker.astype(jnp.bfloat16), scaled, preferred_element_type=jnp.float32
    ).astype(jnp.bfloat16)
    slot_grads = slot_grads.reshape(slot_total, length, channels)
    first_part, second_part = encoder_backward(saved, slot_grads, encoder_first, encoder_second)
    parts = (second_part, first_part, gain_part)
    flat = jnp.concatenate([part.reshape(-1, 128) for part in parts], axis=0)
    flat = jnp.pad(flat, ((0, -flat.shape[0] % 16), (0, 0)))
    grad_kernel, total = outer(grad_pred, gathered, flat)
    sums = []
    at = 0
    for part in parts:
        count = part.size // 128
        sums.append(total[at : at + count].reshape(part.shape))
        at += count
    return (settle(grad_kernel), sums[2], sums[1], sums[0])


def body(
    sar_faces,
    dest_owner,
    face_slot,
    valid_pixels,
    cloud_mask,
    time_index,
    clean_latent,
    noise_latent,
    encoder_first,
    encoder_second,
    conv_kernel,
    norm_gain,
):
    owners = lax.axis_size("tile")
    slot_total = owners * MOST
    face_count, length, channels_in = sar_faces.shape
    rows, columns, channels = clean_latent.shape
    tile_faces = rows * columns // length
    owner_list = dest_owner[:, 0]
    onehot = (owner_list[:, None] == jnp.arange(owners, dtype=jnp.int32)[None, :]).astype(jnp.int32)
    before = jnp.cumsum(onehot, axis=0) - onehot
    within = jnp.sum(before * onehot, axis=1)
    buffer_at = owner_list * MOST + within
    placed = (jnp.arange(slot_total, dtype=jnp.int32)[:, None] == buffer_at[None, :]).astype(
        jnp.int32
    )
    placer = placed.astype(jnp.bfloat16)
    labels = jnp.stack(
        [
            jnp.sum(placed * face_slot[None, :], axis=1),
            jnp.sum(placed * valid_pixels[None, :], axis=1),
        ],
        axis=-1,
    )
    labels = labels.reshape(owners, MOST, 2)
    packed = jnp.einsum(
        "sf,fjc->sjc", placer, sar_faces, preferred_element_type=jnp.float32
    ).astype(jnp.bfloat16)
    arrived, recv_labels = (
        lax.all_to_all(
            packed.reshape(owners, MOST, length, channels_in),
            "tile",
            split_axis=0,
            concat_axis=0,
            tiled=True,
        ),
        lax.all_to_all(labels, "tile", split_axis=0, concat_axis=0, tiled=True),
    )
    raw_slots = arrived.reshape(slot_total, length, channels_in)
    received, saved = encoder_forward(raw_slots, encoder_first, encoder_second)
    recv_labels = recv_labels.reshape(slot_total, 2)
    recv_slot = recv_labels[:, 0]
    recv_count = recv_labels[:, 1]
    validity = (jnp.arange(length, dtype=jnp.int32)[None, :] < recv_count[:, None]).astype(
        jnp.float32
    )
    selector = recv_slot[:, None] == jnp.arange(tile_faces, dtype=jnp.int32)[None, :]
    masked = received * validity[..., None].astype(jnp.bfloat16)
    summed = jnp.einsum(
        "sp,sjc->pjc", selector.astype(jnp.bfloat16), masked, preferred_element_type=jnp.float32
    )
    covered = jnp.einsum(
        "sp,sj->pj", selector.astype(jnp.float32), validity, precision=highest
    ).reshape(-1, 1)
    condition = summed.reshape(-1, channels) / (1.0 + covered)
    time_value = (time_index[0].astype(jnp.float32) + 0.5) / NSTEPS
    noise_flat = noise_latent.astype(jnp.float32).reshape(-1, channels)
    clean_flat = clean_latent.astype(jnp.float32).reshape(-1, channels)
    hsum = (1.0 - time_value) * noise_flat + time_value * clean_flat + condition
    inverse = lax.rsqrt(jnp.mean(hsum * hsum, axis=-1, keepdims=True) + epsilon)
    normed = hsum * inverse
    lifted = normed * norm_gain
    activated = jax.nn.silu(lifted).astype(jnp.bfloat16).reshape(rows, columns, channels)
    extended = with_halo(activated, (("tile", 0),), 1)
    padded = jnp.pad(extended, ((0, 0), (1, 1), (0, 0)))
    predicted = convolve_forward(padded, conv_kernel, rows, columns)
    pixel_weight = (1 + cloud_mask).astype(jnp.float32).reshape(-1, 1)
    grad_pred = (pixel_weight * (predicted - clean_flat + noise_flat) / (rows * columns)).astype(
        jnp.bfloat16
    )
    grad_rows = with_halo(grad_pred.reshape(rows, columns, channels), (("tile", 0),), 1)
    padded_grad = jnp.pad(grad_rows, ((0, 0), (1, 1), (0, 0)))
    flows, kernel_part = convolve_backward(padded, padded_grad, conv_kernel, rows, columns)
    gain_part, grad_hsum = norm_backward(flows, lifted, normed, inverse, norm_gain)
    scaled = (grad_hsum / (1.0 + covered)).reshape(tile_faces, length, channels)
    slot_grads = (jnp.take(scaled, recv_slot, axis=0) * validity[..., None]).astype(jnp.bfloat16)
    first_part, second_part = encoder_backward(saved, slot_grads, encoder_first, encoder_second)
    reduced = lax.psum((kernel_part, gain_part, first_part, second_part), "tile")
    return (reduced[0], reduced[1], reduced[2], reduced[3])


def solution(mesh):
    placed = (
        P(("groups", "tile"), None, None),
        P(("groups", "tile"), None),
        P(("groups", "tile")),
        P(("groups", "tile")),
        P(("groups", "tile"), None),
        P(("groups", "tile")),
        P(("groups", "tile"), None, None),
        P(("groups", "tile"), None, None),
        P(),
        P(),
        P(),
        P(),
    )
    return jax.shard_map(
        body16 if mesh.shape["tile"] == 16 else body,
        mesh=mesh,
        in_specs=placed,
        out_specs=(
            P("groups", None, None),
            P("groups"),
            P("groups", None, None, None),
            P("groups", None, None, None),
        ),
        check_vma=False,
    )
```

```python
import jax
import jax.numpy as jnp
from jax import lax
from jax.experimental import pallas as pl
from jax.experimental.pallas import tpu as pltpu
from jax.sharding import PartitionSpec as P

MOST = 2
NSTEPS = 1000


highest = lax.Precision.HIGHEST
epsilon = 1e-06


def with_halo(block, sides, width):
    for axis, dim in sides:
        count = lax.axis_size(axis)
        forward = [(i, i + 1) for i in range(count - 1)]
        backward = [(target, source) for source, target in forward]
        low = lax.ppermute(
            lax.slice_in_dim(block, block.shape[dim] - width, None, axis=dim), axis, forward
        )
        high = lax.ppermute(lax.slice_in_dim(block, 0, width, axis=dim), axis, backward)
        block = jnp.concatenate([low, block, high], axis=dim)
    return block


def shift_line(values, offset):
    if offset == 0:
        return values
    zeros = jnp.zeros_like(values[:, : abs(offset)])
    if offset > 0:
        return jnp.concatenate([values[:, offset:], zeros], axis=1)
    return jnp.concatenate([zeros, values[:, :offset]], axis=1)


def taps_forward(inputs, weight, spread):
    summed = jnp.zeros(inputs.shape[:3] + (weight.shape[-1],), jnp.float32)
    for shift_tap in range(3):
        shifted = shift_line(inputs, (shift_tap - 1) * spread)
        summed = summed + jnp.einsum(
            "flgi,gio->flgo", shifted, weight[shift_tap], preferred_element_type=jnp.float32
        )
    return summed


def taps_weight_grad(inputs, cotangent, spread, exact):
    pieces = []
    for shift_tap in range(3):
        shifted = shift_line(inputs, (shift_tap - 1) * spread)
        if exact:
            pieces.append(
                jnp.einsum(
                    "flgi,flgo->gio", shifted.astype(jnp.float32), cotangent, precision=highest
                )
            )
        else:
            pieces.append(
                jnp.einsum("flgi,flgo->gio", shifted, cotangent, preferred_element_type=jnp.float32)
            )
    return jnp.stack(pieces)


def taps_input_grad(cotangent, weight, spread):
    summed = jnp.zeros(cotangent.shape[:3] + (weight.shape[2],), jnp.float32)
    for shift_tap in range(3):
        moved = jnp.einsum(
            "flgo,gio->flgi", cotangent, weight[shift_tap], preferred_element_type=jnp.float32
        )
        summed = summed + shift_line(moved, -(shift_tap - 1) * spread)
    return summed


def encoder_forward(sar_faces, first_w, second_w):
    face_count, length, channels_in = sar_faces.shape
    groups = first_w.shape[1]
    inputs = sar_faces.reshape(face_count, length, groups, -1)
    first_out = taps_forward(inputs, first_w, 1)
    hidden = jax.nn.silu(first_out).astype(jnp.bfloat16)
    second = taps_forward(hidden, second_w, 2)
    encoded = (
        (hidden.astype(jnp.float32) + second).reshape(face_count, length, -1).astype(jnp.bfloat16)
    )
    return (encoded, (inputs, first_out, hidden))


def encoder_backward(saved, grad_face, first_w, second_w):
    inputs, first_out, hidden = saved
    groups = first_w.shape[1]
    face_count, length, channels = grad_face.shape
    cotangent = grad_face.reshape(face_count, length, groups, -1)
    second_part = taps_weight_grad(hidden, cotangent, 2, False)
    grad_hidden = cotangent.astype(jnp.float32) + taps_input_grad(cotangent, second_w, 2)
    logistic = jax.nn.sigmoid(first_out)
    grad_first_out = grad_hidden * logistic * (1.0 + first_out * (1.0 - logistic))
    first_part = taps_weight_grad(inputs, grad_first_out, 1, True)
    return (first_part, second_part)


def convolve_forward(padded, kernel, rows, columns):
    channels = kernel.shape[-1]
    summed = jnp.zeros((rows * columns, channels), jnp.float32)
    for row_tap in range(3):
        for col_tap in range(3):
            window = padded[row_tap : row_tap + rows, col_tap : col_tap + columns].reshape(
                -1, channels
            )
            summed = summed + jnp.dot(
                window, kernel[3 * row_tap + col_tap], preferred_element_type=jnp.float32
            )
    return summed


def convolve_backward(padded_act, padded_grad, kernel, rows, columns):
    channels = kernel.shape[-1]
    incoming = padded_grad[1 : rows + 1, 1 : columns + 1].reshape(-1, channels)
    flows = jnp.zeros((rows * columns, channels), jnp.float32)
    kernels = []
    for row_tap in range(3):
        for col_tap in range(3):
            window = padded_act[row_tap : row_tap + rows, col_tap : col_tap + columns].reshape(
                -1, channels
            )
            kernels.append(
                lax.dot_general(
                    window, incoming, (((0,), (0,)), ((), ())), preferred_element_type=jnp.float32
                )
            )
            moved = padded_grad[
                2 - row_tap : 2 - row_tap + rows, 2 - col_tap : 2 - col_tap + columns
            ].reshape(-1, channels)
            flows = flows + lax.dot_general(
                moved,
                kernel[3 * row_tap + col_tap],
                (((1,), (1,)), ((), ())),
                preferred_element_type=jnp.float32,
            )
    return (flows, jnp.stack(kernels))


def norm_backward(flows, lifted, normed, inverse, gain):
    logistic = jax.nn.sigmoid(lifted)
    grad_lift = flows * logistic * (1.0 + lifted * (1.0 - logistic))
    gain_part = jnp.sum(grad_lift * normed, axis=0)
    grad_norm = grad_lift * gain
    grad_hsum = inverse * (
        grad_norm - normed * jnp.mean(grad_norm * normed, axis=-1, keepdims=True)
    )
    return (gain_part, grad_hsum)


MESH = pl.DeviceIdType.MESH
VM = pltpu.VMEM


def entry_barrier(me, count):
    barrier = pltpu.get_barrier_semaphore()
    for k in range(1, count):
        pl.semaphore_signal(
            barrier, inc=1, device_id={"tile": lax.rem(me + k, count)}, device_id_type=MESH
        )
    pl.semaphore_wait(barrier, count - 1)


def exchange_kernel(count, x_ref, o_ref, send, recv, local):
    me = lax.axis_index("tile")
    entry_barrier(me, count)
    own = pltpu.make_async_copy(x_ref.at[me], o_ref.at[me], local)
    own.start()
    copies = []
    for k in range(1, count):
        to = lax.rem(me + k, count)
        copy = pltpu.make_async_remote_copy(
            src_ref=x_ref.at[to],
            dst_ref=o_ref.at[me],
            send_sem=send.at[k - 1],
            recv_sem=recv.at[k - 1],
            device_id={"tile": to},
            device_id_type=MESH,
        )
        copy.start()
        copies.append(copy)
    own.wait()
    for copy in copies:
        copy.wait()


def exchange(packed):
    count = packed.shape[0]
    return pl.pallas_call(
        lambda *refs: exchange_kernel(count, *refs),
        out_shape=jax.ShapeDtypeStruct(packed.shape, packed.dtype),
        in_specs=[pl.BlockSpec(memory_space=VM)],
        out_specs=pl.BlockSpec(memory_space=VM),
        scratch_shapes=[
            pltpu.SemaphoreType.DMA((count - 1,)),
            pltpu.SemaphoreType.DMA((count - 1,)),
            pltpu.SemaphoreType.DMA,
        ],
        compiler_params=pltpu.CompilerParams(collective_id=0, has_side_effects=True),
        name="exchange",
    )(packed)


class Gather:
    def __init__(self, buf, send, recv):
        self.buf, self.send_sem, self.recv_sem = buf, send, recv
        self.me = lax.axis_index("tile")
        self.core = lax.rem(self.me, 2)
        self.x = lax.rem(self.me // 2, 2)
        self.z = z = self.me // 4
        self.x_peer = z * 4 + (1 - self.x) * 2 + self.core
        self.sibling = z * 4 + self.x * 2 + (1 - self.core)
        self.planes = [
            z,
            jnp.where(z == 0, 1, z - 1),
            jnp.where(z == 0, 2, jnp.where(z == 3, 1, z + 1)),
            jnp.where(z < 2, 3, 0),
        ]

    def copy(self, chunk, to, index):
        return pltpu.make_async_remote_copy(
            src_ref=self.buf.at[chunk],
            dst_ref=self.buf.at[chunk],
            send_sem=self.send_sem.at[index],
            recv_sem=self.recv_sem.at[chunk],
            device_id={"tile": to},
            device_id_type=MESH,
        )

    def at(self, step, x, core):
        return self.planes[step] * 4 + x * 2 + core

    def along(self, step):
        place = lax.rem(self.me, 4)
        onward = jnp.where(self.planes[step] < self.z, self.z + 1, self.z - 1)
        valid = (onward >= 0) & (onward <= 3)
        return jnp.clip(onward, 0, 3) * 4 + place, valid

    def start(self):
        place = lax.rem(self.me, 4)

        @pl.when(self.z < 3)
        def _():
            self.copy(self.me, jnp.minimum(self.z + 1, 3) * 4 + place, 0).start()

        @pl.when(self.z > 0)
        def _():
            self.copy(self.me, jnp.maximum(self.z - 1, 0) * 4 + place, 1).start()

        self.copy(self.me, self.x_peer, 2).start()
        self.copy(self.me, self.sibling, 3).start()

    def pass_z(self, step):
        chunk = self.at(step, self.x, self.core)
        self.copy(chunk, self.x_peer, 0).wait_recv()
        to, valid = self.along(step)

        @pl.when(valid)
        def _():
            self.copy(chunk, to, 3 + step).start()

        self.copy(chunk, self.x_peer, 6 + step).start()
        self.copy(chunk, self.sibling, 9 + step).start()

    def pass_x(self, step):
        chunk = self.at(step, 1 - self.x, self.core)
        self.copy(chunk, self.sibling, 0).wait_recv()
        self.copy(chunk, self.sibling, 13 + step).start()

    def take(self, step):
        for x in (self.x, 1 - self.x):
            chunk = self.at(step, x, 1 - self.core)
            self.copy(chunk, self.sibling, 0).wait_recv()

    def drain(self):
        @pl.when(self.z < 3)
        def _():
            self.copy(self.me, self.sibling, 0).wait_send()

        @pl.when(self.z > 0)
        def _():
            self.copy(self.me, self.sibling, 1).wait_send()

        for step in range(1, 4):
            _, valid = self.along(step)

            @pl.when(valid)
            def _():
                self.copy(self.me, self.sibling, 3 + step).wait_send()

        for index in (2, 3, 7, 8, 9, 10, 11, 12, 13, 14, 15, 16):
            self.copy(self.me, self.sibling, index).wait_send()


class Spread:
    def __init__(self, buf, send, recv):
        self.buf, self.send_sem, self.recv_sem = buf, send, recv
        self.me = lax.axis_index("tile")
        self.core = lax.rem(self.me, 2)
        self.x = lax.rem(self.me // 2, 2)
        self.z = self.me // 4
        self.x_peer = self.z * 4 + (1 - self.x) * 2 + self.core
        self.sibling = self.z * 4 + self.x * 2 + (1 - self.core)

    def copy(self, chunk, to, index):
        return pltpu.make_async_remote_copy(
            src_ref=self.buf.at[chunk],
            dst_ref=self.buf.at[chunk],
            send_sem=self.send_sem.at[index],
            recv_sem=self.recv_sem.at[chunk],
            device_id={"tile": to},
            device_id_type=MESH,
        )

    def at(self, back, x, core):
        return lax.rem(self.z + 4 - back, 4) * 4 + x * 2 + core

    def start(self):
        self.copy(self.me, self.x_peer, 3).start()
        self.copy(self.me, self.sibling, 4).start()
        for k in (1, 3, 2):
            to = lax.rem(self.z + k, 4) * 4 + self.x * 2 + self.core
            self.copy(self.me, to, k - 1).start()

    def pass_z(self, back):
        chunk = self.at(back, self.x, self.core)
        self.copy(chunk, self.x_peer, 0).wait_recv()
        self.copy(chunk, self.x_peer, 5 + 2 * (back - 1)).start()
        self.copy(chunk, self.sibling, 6 + 2 * (back - 1)).start()

    def pass_x(self, back):
        chunk = self.at(back, 1 - self.x, self.core)
        self.copy(chunk, self.sibling, 0).wait_recv()
        self.copy(chunk, self.sibling, 11 + back).start()

    def take(self, back):
        for x in (self.x, 1 - self.x):
            chunk = self.at(back, x, 1 - self.core)
            self.copy(chunk, self.sibling, 0).wait_recv()

    def drain(self):
        for index in range(15):
            self.copy(self.me, self.sibling, index).wait_send()


def moved(values, offset, axis):
    extent = values.shape[axis]
    rolled = pltpu.roll(values, (-offset) % extent, axis)
    place = lax.broadcasted_iota(jnp.int32, values.shape, axis)
    return jnp.where(place == (extent - 1 if offset > 0 else 0), 0.0, rolled)


def halo_copies(src, halo, send, recv, me):
    up = pltpu.make_async_remote_copy(
        src_ref=src,
        dst_ref=halo.at[1],
        send_sem=send.at[0],
        recv_sem=recv.at[1],
        device_id={"tile": jnp.maximum(me - 1, 0)},
        device_id_type=MESH,
    )
    down = pltpu.make_async_remote_copy(
        src_ref=src,
        dst_ref=halo.at[0],
        send_sem=send.at[1],
        recv_sem=recv.at[0],
        device_id={"tile": jnp.minimum(me + 1, 15)},
        device_id_type=MESH,
    )
    return up, down


def middle_kernel(
    act_ref,
    clean_ref,
    noise_ref,
    weight_ref,
    kernel_ref,
    flows_ref,
    grad_ref,
    gathered_ref,
    halo_a,
    halo_g,
    gather_send,
    gather_recv,
    a_send,
    a_recv,
    g_send,
    g_recv,
):
    me = lax.axis_index("tile")
    last = 15
    columns = act_ref.shape[0]
    f32 = jnp.float32
    entry_barrier(me, 16)
    a_up, a_down = halo_copies(act_ref, halo_a, a_send, a_recv, me)
    g_up, g_down = halo_copies(grad_ref, halo_g, g_send, g_recv, me)

    @pl.when(me > 0)
    def _():
        a_up.start()

    @pl.when(me < last)
    def _():
        a_down.start()

    gathered_ref[me] = act_ref[...].T
    gather = Spread(gathered_ref, gather_send, gather_recv)
    gather.start()

    @pl.when(me == 0)
    def _():
        halo_a[0] = jnp.zeros_like(halo_a[0])
        halo_g[0] = jnp.zeros_like(halo_g[0])

    @pl.when(me == last)
    def _():
        halo_a[1] = jnp.zeros_like(halo_a[1])
        halo_g[1] = jnp.zeros_like(halo_g[1])

    own = act_ref[...]
    sums = [jnp.dot(own, kernel_ref[3 + d], preferred_element_type=f32) for d in range(3)]

    @pl.when(me > 0)
    def _():
        a_down.wait_recv()

    @pl.when(me < last)
    def _():
        a_up.wait_recv()

    above, below = halo_a[0], halo_a[1]
    sums = [
        sums[d]
        + jnp.dot(above, kernel_ref[d], preferred_element_type=f32)
        + jnp.dot(below, kernel_ref[6 + d], preferred_element_type=f32)
        for d in range(3)
    ]
    predicted = sums[1] + moved(sums[0], -1, 0) + moved(sums[2], 1, 0)
    grad = (
        weight_ref[...]
        * (predicted - clean_ref[...].astype(f32) + noise_ref[...].astype(f32))
        / columns
    ).astype(jnp.bfloat16)
    grad_ref[...] = grad

    @pl.when(me > 0)
    def _():
        g_up.start()

    @pl.when(me < last)
    def _():
        g_down.start()

    def back(values, tap):
        return lax.dot_general(
            values, kernel_ref[tap], (((1,), (1,)), ((), ())), preferred_element_type=f32
        )

    sums = [back(grad, 3 + d) for d in range(3)]
    for k in (1, 3, 2):
        gather.pass_z(k)

    @pl.when(me > 0)
    def _():
        g_down.wait_recv()

    @pl.when(me < last)
    def _():
        g_up.wait_recv()

    above, below = halo_g[0], halo_g[1]
    sums = [sums[d] + back(below, d) + back(above, 6 + d) for d in range(3)]
    flows_ref[...] = sums[1] + moved(sums[0], 1, 0) + moved(sums[2], -1, 0)
    for k in (0, 1, 3, 2):
        gather.pass_x(k)
    for k in (0, 1, 3, 2):
        gather.take(k)
    gather.drain()

    @pl.when(me > 0)
    def _():
        a_up.wait_send()
        g_up.wait_send()

    @pl.when(me < last)
    def _():
        a_down.wait_send()
        g_down.wait_send()


def middle(activated, clean, noise, pixel_weight, kernel):
    pixels, channels = activated.shape
    dma = pltpu.SemaphoreType.DMA
    return pl.pallas_call(
        middle_kernel,
        out_shape=(
            jax.ShapeDtypeStruct((pixels, channels), jnp.float32),
            jax.ShapeDtypeStruct((pixels, channels), jnp.bfloat16),
            jax.ShapeDtypeStruct((16, channels, pixels), jnp.bfloat16),
        ),
        in_specs=[pl.BlockSpec(memory_space=VM)] * 5,
        out_specs=(pl.BlockSpec(memory_space=VM),) * 3,
        scratch_shapes=[
            VM((2, pixels, channels), jnp.bfloat16),
            VM((2, pixels, channels), jnp.bfloat16),
            dma((15,)),
            dma((16,)),
            dma((2,)),
            dma((2,)),
            dma((2,)),
            dma((2,)),
        ],
        compiler_params=pltpu.CompilerParams(
            collective_id=1, has_side_effects=True, vmem_limit_bytes=14 * 2**20
        ),
        name="middle",
    )(activated, clean, noise, pixel_weight, kernel)


def outer_kernel(
    grad_ref,
    gathered_ref,
    parts_ref,
    result_ref,
    total_ref,
    grads,
    shifted,
    sums,
    landed,
    gather_send,
    gather_recv,
    half_send,
    half_recv,
    sum_send,
    sum_recv,
):
    me = lax.axis_index("tile")
    channels, pixels = gathered_ref.shape[1:]
    part = channels // 2
    f32 = jnp.float32
    entry_barrier(me, 16)
    grads[me] = grad_ref[...]
    gather = Gather(grads, gather_send, gather_recv)
    gather.start()
    core, z = gather.core, gather.z
    mine = pl.ds(pl.multiple_of(core * part, part), part)
    rows = parts_ref.shape[0] // 2
    my_rows = pl.ds(pl.multiple_of(core * rows, 8), rows)
    other_rows = pl.ds(pl.multiple_of((1 - core) * rows, 8), rows)
    z_near = (z + 1 - 2 * lax.rem(z, 2)) * 4 + lax.rem(me, 4)
    z_far = lax.rem(z + 2, 4) * 4 + lax.rem(me, 4)

    def sum_copy(src, dst, stage, to):
        return pltpu.make_async_remote_copy(
            src_ref=src,
            dst_ref=dst,
            send_sem=sum_send.at[stage],
            recv_sem=sum_recv.at[stage],
            device_id={"tile": to},
            device_id_type=MESH,
        )

    hops = [
        sum_copy(parts_ref.at[other_rows], landed.at[0], 0, gather.sibling),
        sum_copy(sums.at[0], landed.at[1], 1, gather.x_peer),
        sum_copy(sums.at[1], landed.at[2], 2, z_near),
        sum_copy(sums.at[2], landed.at[3], 3, z_far),
        sum_copy(total_ref.at[my_rows], total_ref.at[my_rows], 4, gather.sibling),
    ]
    hops[0].start()

    def add_hop(stage):
        hops[stage].wait_recv()
        held = parts_ref[my_rows, :] if stage == 0 else sums[stage - 1]
        if stage < 3:
            sums[stage] = held + landed[stage]
        else:
            total_ref[my_rows, :] = held + landed[stage]
        hops[stage + 1].start()

    zeros = jnp.zeros((3 * part, pixels), jnp.bfloat16)
    shifted[:, 0:pixels] = zeros
    shifted[:, 17 * pixels : 18 * pixels] = zeros

    def shift_some(low, high):
        def step(chunk, carry):
            plain = gathered_ref[chunk, mine, :]
            wide = plain.astype(f32)
            here = pl.ds(pl.multiple_of((chunk + 1) * pixels, pixels), pixels)
            shifted[0:part, here] = moved(wide, -1, 1).astype(jnp.bfloat16)
            shifted[part : 2 * part, here] = plain
            shifted[2 * part : 3 * part, here] = moved(wide, 1, 1).astype(jnp.bfloat16)
            return carry

        lax.fori_loop(low, high, step, 0)

    def half_copy(row):
        return pltpu.make_async_remote_copy(
            src_ref=result_ref.at[pl.ds(3 * row, 3), mine],
            dst_ref=result_ref.at[pl.ds(3 * row, 3), mine],
            send_sem=half_send.at[row],
            recv_sem=half_recv.at[row],
            device_id={"tile": gather.sibling},
            device_id_type=MESH,
        )

    def multiply(order):
        base = gather.planes[order] * 4
        right = grads[pl.ds(base, 4)].reshape(4 * pixels, channels)

        def step(row, carry):
            start = pl.multiple_of((base + row) * pixels, pixels)
            left = shifted[:, pl.ds(start, 4 * pixels)]
            product = jnp.dot(left, right, preferred_element_type=f32)
            for d in range(3):
                piece = product[d * part : (d + 1) * part]
                if order == 0:
                    result_ref[3 * row + d, mine, :] = piece
                else:
                    result_ref[3 * row + d, mine, :] = result_ref[3 * row + d, mine, :] + piece
            if order == 3:
                half_copy(row).start()
            return carry

        lax.fori_loop(0, 3, step, 0)

    shift_some(0, 4)
    gather.pass_z(1)
    gather.pass_x(0)
    add_hop(0)
    shift_some(4, 10)
    gather.pass_z(2)
    gather.pass_x(1)
    shift_some(10, 16)
    add_hop(1)
    gather.take(0)
    gather.pass_z(3)
    multiply(0)
    gather.pass_x(2)
    add_hop(2)
    gather.take(1)
    multiply(1)
    gather.pass_x(3)
    add_hop(3)
    gather.take(2)
    multiply(2)
    gather.take(3)
    multiply(3)
    hops[4].wait_recv()
    gather.drain()
    for hop in hops:
        hop.wait_send()
    for row in range(3):
        half_copy(row).wait()


def outer(grad, gathered, parts):
    pixels, channels = grad.shape
    rows = parts.shape[0] // 2
    dma = pltpu.SemaphoreType.DMA
    return pl.pallas_call(
        outer_kernel,
        out_shape=(
            jax.ShapeDtypeStruct((9, channels, channels), jnp.float32),
            jax.ShapeDtypeStruct(parts.shape, jnp.float32),
        ),
        in_specs=[pl.BlockSpec(memory_space=VM)] * 3,
        out_specs=(pl.BlockSpec(memory_space=VM),) * 2,
        scratch_shapes=[
            VM((16, pixels, channels), jnp.bfloat16),
            VM((3 * channels // 2, 18 * pixels), jnp.bfloat16),
            VM((3, rows, 128), jnp.float32),
            VM((4, rows, 128), jnp.float32),
            dma((17,)),
            dma((16,)),
            dma((3,)),
            dma((3,)),
            dma((5,)),
            dma((5,)),
        ],
        compiler_params=pltpu.CompilerParams(
            collective_id=2, has_side_effects=True, vmem_limit_bytes=24 * 2**20
        ),
        name="outer",
    )(grad, gathered, parts)


def settle_kernel(x_ref, o_ref):
    o_ref[...] = x_ref[...]


def settle(values):
    taps, rows, columns = values.shape
    block = pl.BlockSpec((1, rows, columns), lambda i: (i, 0, 0))
    return pl.pallas_call(
        settle_kernel,
        grid=(taps,),
        out_shape=jax.ShapeDtypeStruct(values.shape, values.dtype),
        in_specs=[block],
        out_specs=block,
        name="settle",
    )(values)


def body16(
    sar_faces,
    dest_owner,
    face_slot,
    valid_pixels,
    cloud_mask,
    time_index,
    clean_latent,
    noise_latent,
    encoder_first,
    encoder_second,
    conv_kernel,
    norm_gain,
):
    owners = lax.axis_size("tile")
    slot_total = owners * MOST
    face_count, length, channels_in = sar_faces.shape
    rows, columns, channels = clean_latent.shape
    tile_faces = rows * columns // length
    owner_list = dest_owner[:, 0]
    onehot = (owner_list[:, None] == jnp.arange(owners, dtype=jnp.int32)[None, :]).astype(jnp.int32)
    before = jnp.cumsum(onehot, axis=0) - onehot
    within = jnp.sum(before * onehot, axis=1)
    buffer_at = owner_list * MOST + within
    placed = (jnp.arange(slot_total, dtype=jnp.int32)[:, None] == buffer_at[None, :]).astype(
        jnp.int32
    )
    placer = placed.astype(jnp.bfloat16)
    labels = jnp.stack(
        [
            jnp.sum(placed * face_slot[None, :], axis=1),
            jnp.sum(placed * valid_pixels[None, :], axis=1),
        ],
        axis=-1,
    )
    packed = jnp.einsum(
        "sf,fjc->sjc", placer, sar_faces, preferred_element_type=jnp.float32
    ).astype(jnp.bfloat16)
    label_rows = jnp.pad(
        labels.astype(jnp.bfloat16)[:, None, :],
        ((0, 0), (0, length - 1), (0, channels_in - 2)),
    )
    arrived = exchange(
        jnp.concatenate([packed, label_rows], axis=1).reshape(
            owners, MOST * 2 * length, channels_in
        )
    ).reshape(slot_total, 2 * length, channels_in)
    raw_slots = arrived[:, :length]
    recv_labels = arrived[:, length, :2].astype(jnp.int32)
    received, saved = encoder_forward(raw_slots, encoder_first, encoder_second)
    recv_slot = recv_labels[:, 0]
    recv_count = recv_labels[:, 1]
    validity = (jnp.arange(length, dtype=jnp.int32)[None, :] < recv_count[:, None]).astype(
        jnp.float32
    )
    selector = recv_slot[:, None] == jnp.arange(tile_faces, dtype=jnp.int32)[None, :]
    masked = received * validity[..., None].astype(jnp.bfloat16)
    summed = jnp.einsum(
        "sp,sjc->pjc", selector.astype(jnp.bfloat16), masked, preferred_element_type=jnp.float32
    )
    covered = jnp.einsum(
        "sp,sj->pj", selector.astype(jnp.float32), validity, precision=highest
    ).reshape(-1, 1)
    condition = summed.reshape(-1, channels) / (1.0 + covered)
    time_value = (time_index[0].astype(jnp.float32) + 0.5) / NSTEPS
    noise_flat = noise_latent.astype(jnp.float32).reshape(-1, channels)
    clean_flat = clean_latent.astype(jnp.float32).reshape(-1, channels)
    hsum = (1.0 - time_value) * noise_flat + time_value * clean_flat + condition
    inverse = lax.rsqrt(jnp.mean(hsum * hsum, axis=-1, keepdims=True) + epsilon)
    normed = hsum * inverse
    lifted = normed * norm_gain
    activated = jax.nn.silu(lifted).astype(jnp.bfloat16)
    pixel_weight = (1 + cloud_mask).astype(jnp.float32).reshape(-1, 1)
    flows, grad_pred, gathered = middle(
        activated,
        clean_latent.reshape(-1, channels),
        noise_latent.reshape(-1, channels),
        pixel_weight,
        conv_kernel,
    )
    gain_part, grad_hsum = norm_backward(flows, lifted, normed, inverse, norm_gain)
    scaled = (grad_hsum / (1.0 + covered)).astype(jnp.bfloat16)
    target = recv_slot[:, None] * length + jnp.arange(length, dtype=jnp.int32)[None, :]
    target = jnp.where(validity > 0, target, -1).reshape(-1)
    picker = target[:, None] == jnp.arange(rows * columns, dtype=jnp.int32)[None, :]
    slot_grads = jnp.dot(
        picker.astype(jnp.bfloat16), scaled, preferred_element_type=jnp.float32
    ).astype(jnp.bfloat16)
    slot_grads = slot_grads.reshape(slot_total, length, channels)
    first_part, second_part = encoder_backward(saved, slot_grads, encoder_first, encoder_second)
    parts = (second_part, first_part, gain_part)
    flat = jnp.concatenate([part.reshape(-1, 128) for part in parts], axis=0)
    flat = jnp.pad(flat, ((0, -flat.shape[0] % 16), (0, 0)))
    grad_kernel, total = outer(grad_pred, gathered, flat)
    sums = []
    at = 0
    for part in parts:
        count = part.size // 128
        sums.append(total[at : at + count].reshape(part.shape))
        at += count
    return (settle(grad_kernel), sums[2], sums[1], sums[0])


def body(
    sar_faces,
    dest_owner,
    face_slot,
    valid_pixels,
    cloud_mask,
    time_index,
    clean_latent,
    noise_latent,
    encoder_first,
    encoder_second,
    conv_kernel,
    norm_gain,
):
    owners = lax.axis_size("tile")
    slot_total = owners * MOST
    face_count, length, channels_in = sar_faces.shape
    rows, columns, channels = clean_latent.shape
    tile_faces = rows * columns // length
    owner_list = dest_owner[:, 0]
    onehot = (owner_list[:, None] == jnp.arange(owners, dtype=jnp.int32)[None, :]).astype(jnp.int32)
    before = jnp.cumsum(onehot, axis=0) - onehot
    within = jnp.sum(before * onehot, axis=1)
    buffer_at = owner_list * MOST + within
    placed = (jnp.arange(slot_total, dtype=jnp.int32)[:, None] == buffer_at[None, :]).astype(
        jnp.int32
    )
    placer = placed.astype(jnp.bfloat16)
    labels = jnp.stack(
        [
            jnp.sum(placed * face_slot[None, :], axis=1),
            jnp.sum(placed * valid_pixels[None, :], axis=1),
        ],
        axis=-1,
    )
    labels = labels.reshape(owners, MOST, 2)
    packed = jnp.einsum(
        "sf,fjc->sjc", placer, sar_faces, preferred_element_type=jnp.float32
    ).astype(jnp.bfloat16)
    arrived, recv_labels = (
        lax.all_to_all(
            packed.reshape(owners, MOST, length, channels_in),
            "tile",
            split_axis=0,
            concat_axis=0,
            tiled=True,
        ),
        lax.all_to_all(labels, "tile", split_axis=0, concat_axis=0, tiled=True),
    )
    raw_slots = arrived.reshape(slot_total, length, channels_in)
    received, saved = encoder_forward(raw_slots, encoder_first, encoder_second)
    recv_labels = recv_labels.reshape(slot_total, 2)
    recv_slot = recv_labels[:, 0]
    recv_count = recv_labels[:, 1]
    validity = (jnp.arange(length, dtype=jnp.int32)[None, :] < recv_count[:, None]).astype(
        jnp.float32
    )
    selector = recv_slot[:, None] == jnp.arange(tile_faces, dtype=jnp.int32)[None, :]
    masked = received * validity[..., None].astype(jnp.bfloat16)
    summed = jnp.einsum(
        "sp,sjc->pjc", selector.astype(jnp.bfloat16), masked, preferred_element_type=jnp.float32
    )
    covered = jnp.einsum(
        "sp,sj->pj", selector.astype(jnp.float32), validity, precision=highest
    ).reshape(-1, 1)
    condition = summed.reshape(-1, channels) / (1.0 + covered)
    time_value = (time_index[0].astype(jnp.float32) + 0.5) / NSTEPS
    noise_flat = noise_latent.astype(jnp.float32).reshape(-1, channels)
    clean_flat = clean_latent.astype(jnp.float32).reshape(-1, channels)
    hsum = (1.0 - time_value) * noise_flat + time_value * clean_flat + condition
    inverse = lax.rsqrt(jnp.mean(hsum * hsum, axis=-1, keepdims=True) + epsilon)
    normed = hsum * inverse
    lifted = normed * norm_gain
    activated = jax.nn.silu(lifted).astype(jnp.bfloat16).reshape(rows, columns, channels)
    extended = with_halo(activated, (("tile", 0),), 1)
    padded = jnp.pad(extended, ((0, 0), (1, 1), (0, 0)))
    predicted = convolve_forward(padded, conv_kernel, rows, columns)
    pixel_weight = (1 + cloud_mask).astype(jnp.float32).reshape(-1, 1)
    grad_pred = (pixel_weight * (predicted - clean_flat + noise_flat) / (rows * columns)).astype(
        jnp.bfloat16
    )
    grad_rows = with_halo(grad_pred.reshape(rows, columns, channels), (("tile", 0),), 1)
    padded_grad = jnp.pad(grad_rows, ((0, 0), (1, 1), (0, 0)))
    flows, kernel_part = convolve_backward(padded, padded_grad, conv_kernel, rows, columns)
    gain_part, grad_hsum = norm_backward(flows, lifted, normed, inverse, norm_gain)
    scaled = (grad_hsum / (1.0 + covered)).reshape(tile_faces, length, channels)
    slot_grads = (jnp.take(scaled, recv_slot, axis=0) * validity[..., None]).astype(jnp.bfloat16)
    first_part, second_part = encoder_backward(saved, slot_grads, encoder_first, encoder_second)
    reduced = lax.psum((kernel_part, gain_part, first_part, second_part), "tile")
    return (reduced[0], reduced[1], reduced[2], reduced[3])


def solution(mesh):
    placed = (
        P(("groups", "tile"), None, None),
        P(("groups", "tile"), None),
        P(("groups", "tile")),
        P(("groups", "tile")),
        P(("groups", "tile"), None),
        P(("groups", "tile")),
        P(("groups", "tile"), None, None),
        P(("groups", "tile"), None, None),
        P(),
        P(),
        P(),
        P(),
    )
    return jax.shard_map(
        body16 if mesh.shape["tile"] == 16 else body,
        mesh=mesh,
        in_specs=placed,
        out_specs=(
            P("groups", None, None),
            P("groups"),
            P("groups", None, None, None),
            P("groups", None, None, None),
        ),
        check_vma=False,
    )
```
